32 devices in a mesh: seg: 8 (over z, x), grp: 4 (over y, core).
Axes of the slice: x: 2, y: 2, z: 4, core: 2. Of those that a mesh axis runs over, the one named last changes fastest.
Arguments:
- initial_state: float32 [512], replicated, may hold values from -6 to 6
- transition: float32 [512, 512], replicated, as said below
- gains: float32 [512], replicated, may hold values from 0 to 1, as said below
- tiles: float32 [4, 4096, 512], P('grp', 'seg'), may hold values from -16 to 16
- tile_owner: int32 [4, 4096, 1], P('grp', 'seg'), may hold values from 0 to 31; in each aligned block of 512 rows (0 to 511, 512 to 1023, ..., all dimensions but the last counted through in order) at most 40 rows name the same one
- tile_step: int32 [4, 4096], P('grp', 'seg'), may hold values from 0 to 31
Outputs:
- states: float32 [4, 256, 512], P('grp', 'seg')
The draws below stay inside these ranges and needn't reach their ends.
Inputs may be any that keep to these rules, and one draw needn't show every extreme that they name: `tile_owner`: among the tiles of one device no owner is named more than 40 times, and in some devices one owner is named exactly 40 times. `transition`: diagonal entries lie strictly between 0 and 1. `gains`: every gain is positive.
All inputs are finite; a program needn't handle non-finite values.
Results may differ from the reference program's by a relative error of at most 0.0003.
Values sent between devices are 32-bit elements; how exact they have to be, the bound alone decides.
A program may use at most 192 MiB of HBM per device.

```python
import math
import jax
import jax.numpy as jnp
import numpy as np
from jax import lax

W = 512
STEP_DEV = 32
TILE_DEV = 512
CAP = 40
STEPS = 1024
TILES = 16384
N_SEG = 8
N_GRP = 4


def mode_pick(key):
    return jax.random.randint(jax.random.fold_in(key, 11), (W,), 0, 8)


def log_between(key, lower, upper):
    unit = jax.random.uniform(key, (W,), jnp.float32)
    return jnp.exp(math.log(lower) + unit * (math.log(upper) - math.log(lower)))


def signed_hadamard(key):
    row_ids = jnp.arange(W, dtype=jnp.int32)
    column_order = jax.random.permutation(jax.random.fold_in(key, 1), W).astype(jnp.int32)
    common_bits = jnp.bitwise_and(row_ids[:, None], column_order[None, :])
    parity = jnp.zeros((W, W), jnp.int32)
    for bit_place in range(W.bit_length()):
        parity = parity + jnp.bitwise_and(jnp.right_shift(common_bits, bit_place), 1)
    row_signs = 2 * jax.random.randint(jax.random.fold_in(key, 2), (W,), 0, 2) - 1
    column_signs = 2 * jax.random.randint(jax.random.fold_in(key, 3), (W,), 0, 2) - 1
    sign_table = (1 - 2 * (parity % 2)) * row_signs[:, None] * column_signs[None, :]
    return sign_table.astype(jnp.float32) * (1.0 / math.sqrt(W))


def draw_transition(key, part):
    slow = mode_pick(key) < 4
    first_share = 0.5
    slow_rate = log_between(jax.random.fold_in(key, 21), 0.1 / STEPS, 0.5 / STEPS)
    fast_rate = log_between(jax.random.fold_in(key, 22), 0.01, 0.03)
    diagonal = jnp.exp(-jnp.where(slow, slow_rate, fast_rate))
    mixing = 4.0 / max(STEPS, 1024)
    first_table = signed_hadamard(jax.random.fold_in(key, 23))
    second_table = signed_hadamard(jax.random.fold_in(key, 24))
    rotation = first_share * (first_table - first_table.T) + (1.0 - first_share) * (second_table - second_table.T)
    identity = jnp.eye(W, dtype=jnp.float32)
    blended = identity + mixing * rotation
    return diagonal[:, None] * blended


def draw_gains(key, part):
    slow = mode_pick(key) < 4
    per_step = STEP_DEV / TILE_DEV
    slow_gain = log_between(jax.random.fold_in(key, 31), 0.1 / TILES, 0.4 / TILES)
    fast_gain = log_between(jax.random.fold_in(key, 32), 0.01 * per_step, 0.1 * per_step)
    return jnp.where(slow, slow_gain, fast_gain)


def set_ends(result, stream_key, least, high):
    shape = result.shape
    spot = [jax.random.randint(jax.random.fold_in(stream_key, axis), (), 0, shape[axis]) for axis in range(len(shape))]
    result = result.at[tuple(spot)].set(least)
    longest = shape.index(max(shape))
    spot[longest] = (spot[longest] + 1) % shape[longest]
    return result.at[tuple(spot)].set(high)


def block_scale(own_key, extent, shards, least, high):
    level = 1.0
    for axis_at, shards_of in shards:
        steps = jax.random.uniform(jax.random.fold_in(jax.random.fold_in(own_key, 6), axis_at), (shards_of,), jnp.float32, least / len(shards), high / len(shards))
        level = level * jnp.repeat(jnp.exp(steps), extent[axis_at] // shards_of).reshape((-1,) + (1,) * (len(extent) - 1 - axis_at))
    return level


def rank_bounds(amount, lean):
    loads = [(1 << 20) // math.isqrt(standing ** lean) + 1 for standing in range(1, amount + 1)]
    scale = 1 + sum(loads) // (1 << 30)
    return np.cumsum(np.array([max(1, weight // scale) for weight in loads]))


def ranked_ids(rng, shape, count, lean):
    table = rank_bounds(count, lean)
    lot = jax.random.randint(jax.random.fold_in(rng, 1), shape, 0, int(table[count - 1]))
    rank = jnp.searchsorted(jnp.asarray(table, jnp.int32), lot, side="right")
    return jax.random.permutation(jax.random.fold_in(rng, 2), count)[rank].astype(jnp.int32)


def routed_block(stream_key, own, number, rows, amount, top, bound, slope):
    order = jax.random.permutation(stream_key, amount)
    crowded, ordinary = portions_of(amount, rows * top, bound, slope, True), portions_of(amount, rows * top, bound, slope, False)
    places = jnp.arange(amount)

    def named(sizes, offset_by):
        used = int((sizes > 0).sum())
        fixed = max(1, used // 4)
        shifted = fixed + (places - fixed + offset_by * (used - fixed)) % max(1, amount - fixed)
        return jnp.zeros((amount,), jnp.int32).at[order[jnp.where(places < fixed, places, shifted)]].set(jnp.asarray(sizes, jnp.int32))

    sizes = jnp.where(number % 4 == 0, named(crowded, number // 4), named(ordinary, number - number // 4 - 1))
    mixed = jax.random.permutation(jax.random.fold_in(own, 3), amount)
    source_of, receiver = mixed[0:amount // 2 * 2:2], mixed[1:amount // 2 * 2:2]
    room = jnp.minimum(sizes[source_of] - 1, bound - sizes[receiver]) // 2
    room = jnp.where((source_of == order[0]) | (receiver == order[0]) | (sizes[receiver] == 0), 0, jnp.maximum(room, 0))
    shifted = jax.random.randint(jax.random.fold_in(own, 4), (amount // 2,), 0, 1 << 20) % (room + 1)
    sizes = sizes.at[source_of].add(-shifted).at[receiver].add(shifted)
    members = jnp.searchsorted(jnp.cumsum(sizes), jnp.arange(rows * top), side="right").astype(jnp.int32)
    table = members.reshape(top, rows).T
    table = table[jax.random.permutation(jax.random.fold_in(own, 1), rows)]
    offset_by = jax.random.randint(jax.random.fold_in(own, 2), (rows, 1), 0, top)
    return jnp.take_along_axis(table, (jnp.arange(top)[None, :] + offset_by) % top, axis=1)


def portions_of(count, total, most, lean, full):
    portions = [(1 << 20) // math.isqrt(grade ** lean) + 1 for grade in range(1, count + 1)]
    largest = most if full else min(most, max(-(-total // count), total * portions[0] // sum(portions)))
    least = 1 if total - largest >= count - 1 else 0
    holding, rest = [largest] + [least] * (count - 1), total - largest - least * (count - 1)
    while rest > 0:
        candidates = [i for i in range(1, count) if holding[i] < largest] or [i for i in range(1, count) if holding[i] < most]
        mass, remaining = sum([portions[i] for i in candidates]), rest
        for i in candidates:
            addition = min(most - holding[i], max(1, remaining * portions[i] // mass), rest)
            holding[i] = holding[i] + addition
            rest = rest - addition
    return np.array(holding)


def noise(own_key, dims, scale, limit, pieces=(), kind=jnp.bfloat16):
    array = jax.random.normal(own_key, dims, jnp.float32) * scale
    if len(pieces) > 0:
        array = block_scale(own_key, dims, pieces, -0.22, 0.18) * array
    return jnp.clip(array, min=-limit, max=limit).astype(kind)


def setup_inputs(seed: int = 0) -> dict:
    splits = jax.random.split(jax.random.key(seed), 7)
    initial_state = noise(splits[0], (W,), 1.0, 6.0, (), jnp.float32)
    transition = draw_transition(jax.random.fold_in(splits[6], 71), 0)
    gains = draw_gains(jax.random.fold_in(splits[6], 71), 0)
    tiles = noise(splits[3], (N_GRP, N_SEG * TILE_DEV, W), 4.0, 16.0, ((0, 4), (1, 8)), jnp.float32)
    tile_owner_keys = jax.random.split(jax.random.fold_in(splits[4], 1), N_GRP * (N_SEG * TILE_DEV) // TILE_DEV)
    tile_owner_turns = jax.random.permutation(jax.random.fold_in(splits[4], 3), N_GRP * (N_SEG * TILE_DEV) // TILE_DEV)
    tile_owner = jax.vmap(lambda own, number: routed_block(jax.random.fold_in(splits[4], 2), own, number, TILE_DEV, N_SEG * N_GRP, 1, CAP, 2))(tile_owner_keys, tile_owner_turns).reshape((N_GRP, N_SEG * TILE_DEV, 1))
    tile_step = set_ends(ranked_ids(splits[5], (N_GRP, N_SEG * TILE_DEV), STEP_DEV, 3), jax.random.fold_in(splits[5], 3), 0, STEP_DEV - 1).astype(jnp.int32)
    return {"initial_state": initial_state, "transition": transition, "gains": gains, "tiles": tiles, "tile_owner": tile_owner, "tile_step": tile_step}


def reference(initial_state, transition, gains, tiles, tile_owner, tile_step):
    width = transition.shape[0]
    flat_rows = tiles.reshape(-1, width)
    where_step = (tile_owner.reshape(-1) * STEP_DEV + tile_step.reshape(-1)).astype(jnp.int32)
    obs_sum = jax.ops.segment_sum(flat_rows, where_step, num_segments=STEPS)
    obs_count = jax.ops.segment_sum(jnp.ones(where_step.shape, jnp.float32), where_step, num_segments=STEPS)
    scale = 1.0 / (1.0 + obs_count[:, None] * gains[None, :])

    def advance(state, inputs):
        sums, factor = inputs
        moved = jnp.dot(transition, state, precision=lax.Precision.HIGHEST)
        following = factor * (moved + gains * sums)
        return following, following

    final_state, states = lax.scan(advance, initial_state, (obs_sum, scale))
    return states.reshape(N_GRP, N_SEG * STEP_DEV, width)
```

```python
import functools

import jax
import jax.numpy as jnp
import numpy as np
from jax import lax
from jax.experimental import pallas as pl
from jax.experimental.pallas import tpu as pltpu
from jax.sharding import PartitionSpec as P

STEP_DEV = 32
LEAST = (48, 56, 64, 72)
EXTRA = 8
DEPTH = len(LEAST)
LONGEST = max(LEAST) + EXTRA
COLUMN = DEPTH * 2 * STEP_DEV
PIECE = 8
PARTS = ((0, 112), (112, 208)), ((208, 368), (368, 512))
SHARE = PARTS[0][-1][1]
FIRST = 7
BEFORE_LINE = 2
TABLED = 4

F32 = jnp.float32
BF16 = jnp.bfloat16
VMEM = pl.BlockSpec(memory_space=pltpu.VMEM)


class Layout:
    def __init__(self, n_seg, n_grp):
        self.n_seg, self.n_grp = n_seg, n_grp
        self.n_chip = n_seg * n_grp // 2
        self.n_plane = self.n_chip // DEPTH
        self.core_in_seg = n_seg // DEPTH > n_grp
        self.n_x = n_seg // DEPTH // (2 if self.core_in_seg else 1)

    def turn(self, level, at):
        return at + (self.n_plane - 1 - 2 * at) * (level % 2)

    def device(self, level, spot, core):
        y, x = spot // self.n_x, spot % self.n_x
        x = x + (self.n_x - 1 - 2 * x) * (y % 2)
        if self.core_in_seg:
            return {"seg": (level * self.n_x + x) * 2 + core, "grp": y}
        return {"seg": level * self.n_x + x, "grp": y * 2 + core}

    def chip(self, q, core):
        level = q // self.n_plane
        return self.device(level, self.turn(level, q % self.n_plane), core)

    def here(self, seg, grp):
        if self.core_in_seg:
            core, y, across = seg % 2, grp, seg // 2
        else:
            core, y, across = grp % 2, grp // 2, seg
        level, x = across // self.n_x, across % self.n_x
        x = x + (self.n_x - 1 - 2 * x) * (y % 2)
        return level, y * self.n_x + x, core

    def late(self, at):
        return (2 * at) // self.n_plane

    def length(self, level, at):
        return pick(LEAST, level) + EXTRA * self.late(at)

    def first_step(self, level, at):
        starts = [sum(LEAST[:z]) * self.n_plane + z * EXTRA * self.n_plane // 2 for z in range(DEPTH)]
        return pick(starts, level) + at * pick(LEAST, level) + EXTRA * self.late(at) * (at - self.n_plane // 2)

    def column_start(self, level, spot):
        late = self.late(spot)
        return sum(LEAST[z] + EXTRA * (late if z % 2 == 0 else 1 - late) for z in range(level))


def pick(table, index):
    if isinstance(index, int):
        return table[index]
    return table[0] + sum((table[at] - table[0]) * (index == at).astype(jnp.int32) for at in range(1, len(table)))


def split(value):
    upper = value.astype(BF16)
    return upper, (value - upper.astype(F32)).astype(BF16)


def product(upper, lower, right_upper, right_lower):
    dot = functools.partial(jnp.dot, preferred_element_type=F32)
    return dot(upper, right_upper) + dot(lower, right_upper) + dot(upper, right_lower)


def row_times(row, matrix_ref):
    depth, width = matrix_ref.shape
    column = jnp.transpose(jnp.broadcast_to(row, (128, depth)))
    return jnp.concatenate(
        [
            jnp.sum(matrix_ref[:, at : at + 128] * column, axis=0, keepdims=True)
            for at in range(0, width, 128)
        ],
        axis=1,
    )


def filter_kernel(
    lay,
    initial_ref,
    transition_ref,
    moved_ref,
    gains_ref,
    counts_ref,
    where_ref,
    tiles_ref,
    out_ref,
    upper_ref,
    lower_ref,
    map_ref,
    scale_ref,
    column_ref,
    gains_column_ref,
    factors_ref,
    drive_ref,
    drive_columns_ref,
    between_ref,
    states_ref,
    final_ref,
    mate_tiles_ref,
    mate_where_ref,
    tile_upper_ref,
    tile_lower_ref,
    counts_in_ref,
    plane_out_ref,
    plane_in_ref,
    plane_sum_ref,
    line_in_ref,
    into_ref,
    send_ref,
    shift_ref,
    shift_in_ref,
    counts_sems,
    mate_sems,
    plane_sems,
    line_send_sems,
    line_sem,
    share_sems,
    shift_sems,
    into_sem,
    send_sems,
    piece_sems,
    final_sem,
):
    n_seg, n_grp = lay.n_seg, lay.n_grp
    n_dev, n_plane, n_chip = n_seg * n_grp, lay.n_plane, lay.n_chip
    seg, grp = lax.axis_index("seg"), lax.axis_index("grp")
    level, spot, core = lay.here(seg, grp)
    at_level = lay.turn(level, spot)
    q = level * n_plane + at_level
    me = q * 2 + core
    length = lay.length(level, at_level)
    start = lay.first_step(level, at_level)
    groups = length // 8
    width = map_ref.shape[1]
    tile_count = tiles_ref.shape[0]
    barrier = pltpu.get_barrier_semaphore()

    def greet(at, carry):
        other = (me + 1 + at) % n_dev
        pl.semaphore_signal(barrier, inc=1, device_id=lay.chip(other // 2, other % 2))
        return carry

    lax.fori_loop(0, n_dev - 1, greet, 0)

    row_ids = lax.broadcasted_iota(jnp.int32, (width, width), 0)
    column_ids = lax.broadcasted_iota(jnp.int32, (width, width), 1)
    on_diagonal = row_ids == column_ids
    diagonal = jnp.sum(jnp.where(on_diagonal, moved_ref[...], 0.0), axis=0, keepdims=True)
    upper, lower = split(jnp.where(on_diagonal, 0.0, moved_ref[...]))
    upper_ref[...] = upper
    lower_ref[...] = lower
    pl.semaphore_wait(barrier, n_dev - 1)

    def landed(ref, sem):
        pltpu.make_async_copy(ref, ref, sem).wait()

    def mate_copies():
        return [
            pltpu.make_async_remote_copy(
                src_ref=source,
                dst_ref=target,
                send_sem=mate_sems.at[2 * at],
                recv_sem=mate_sems.at[2 * at + 1],
                device_id=lay.device(level, spot, 0),
            )
            for at, (source, target) in enumerate(
                ((tiles_ref, mate_tiles_ref), (where_ref, mate_where_ref))
            )
        ]

    @pl.when(core == 1)
    def _():
        for copy in mate_copies():
            copy.start()

    def send_counts(at, carry):
        other = (me + 1 + at) % n_dev
        pltpu.make_async_remote_copy(
            src_ref=counts_ref.at[other // 2],
            dst_ref=counts_in_ref.at[at],
            send_sem=counts_sems.at[0],
            recv_sem=counts_sems.at[1],
            device_id=lay.chip(other // 2, other % 2),
        ).start()
        return carry

    lax.fori_loop(0, n_dev - 1, send_counts, 0)

    def binned(column):
        rows = lax.broadcasted_iota(jnp.int32, (COLUMN, 1), 0)
        steps = rows
        for z in range(DEPTH):
            begin = lay.column_start(z, column)
            moved_by = lay.first_step(z, lay.turn(z, column)) - begin
            steps = rows + moved_by if z == 0 else jnp.where(rows >= begin, rows + moved_by, steps)
        where = jnp.concatenate([where_ref[...], mate_where_ref[...]], axis=1)
        placed = (steps == where).astype(F32).astype(BF16)
        dot = functools.partial(jnp.dot, preferred_element_type=F32)
        return dot(placed, tile_upper_ref[...]) + dot(placed, tile_lower_ref[...])

    def send_plane(at, carry):
        other = (spot + 1 + at) % n_plane
        plane_out_ref[at] = binned(other)
        pltpu.make_async_remote_copy(
            src_ref=plane_out_ref.at[at],
            dst_ref=plane_in_ref.at[at],
            send_sem=plane_sems.at[0],
            recv_sem=plane_sems.at[1],
            device_id=lay.device(level, other, 0),
        ).start()
        return carry

    @pl.when(core == 0)
    def _():
        upper, lower = split(tiles_ref[...])
        tile_upper_ref[0:tile_count] = upper
        tile_lower_ref[0:tile_count] = lower
        for copy in mate_copies():
            copy.wait_recv()
        upper, lower = split(mate_tiles_ref[...])
        tile_upper_ref[tile_count:] = upper
        tile_lower_ref[tile_count:] = lower
        lax.fori_loop(0, n_plane - 1, send_plane, 0)
        plane_sum_ref[0:COLUMN] = binned(spot)
        plane_sum_ref[COLUMN:] = jnp.zeros((EXTRA, width), F32)
        gains_column_ref[...] = jnp.transpose(jnp.broadcast_to(gains_ref[...], (128, width)))

    landed(counts_in_ref, counts_sems.at[1])
    counts = counts_ref[q] + jnp.sum(counts_in_ref[...], axis=0)
    column = jnp.transpose(jnp.broadcast_to(counts, (128, 128)))[:LONGEST]
    for at in range(0, width, 128):
        scale_ref[:, at : at + 128] = 1.0 / (1.0 + column * gains_ref[:, at : at + 128])
    column_ref[...] = column

    def tabulate(entry):
        count = column_ref[pl.ds(2 * entry, 1), :]
        factors_ref[entry] = 1.0 / (1.0 + count * gains_column_ref[...])

    def advance_maps(parts, first, count, tabled):
        values = [map_ref[begin:end, :] for begin, end in parts]
        for ahead in range(count):
            factor = scale_ref[pl.ds(first + ahead, 1), :]
            for at, value in enumerate(values):
                upper, lower = split(value)
                joined = product(upper, lower, upper_ref[...], lower_ref[...])
                values[at] = (joined + value * diagonal) * factor
            if tabled:
                tabulate(first + ahead - 1)
        for (begin, end), value in zip(parts, values):
            map_ref[begin:end, :] = value

    def start_maps(parts, tabled):
        for begin, end in parts:
            map_ref[begin:end, :] = moved_ref[begin:end, :] * scale_ref[pl.ds(0, 1), :]
        advance_maps(parts, 1, FIRST, tabled)

    def map_groups(parts, begin, end, tabled):
        def group(at, carry):
            advance_maps(parts, 8 * at, 8, tabled)
            return carry

        lax.fori_loop(begin, end, group, 0)

    is_middle = jnp.logical_and(q > 0, q < n_chip - 1)

    def chain_copies(q_next):
        return [
            pltpu.make_async_remote_copy(
                src_ref=send_ref,
                dst_ref=into_ref,
                send_sem=send_sems.at[other],
                recv_sem=into_sem,
                device_id=lay.chip(q_next, other),
            )
            for other in (1, 0)
        ]

    share_ref = map_ref.at[0:SHARE]

    def share_copy():
        return pltpu.make_async_remote_copy(
            src_ref=share_ref,
            dst_ref=share_ref,
            send_sem=share_sems.at[0],
            recv_sem=share_sems.at[1],
            device_id=lay.device(level, spot, 1),
        )

    def shift_copy():
        return pltpu.make_async_remote_copy(
            src_ref=shift_ref,
            dst_ref=shift_in_ref,
            send_sem=shift_sems.at[0],
            recv_sem=shift_sems.at[1],
            device_id=lay.device(level, spot, 1),
        )

    lanes = lax.broadcasted_iota(jnp.int32, (width, 128), 1)

    def two_steps(at, row):
        moved = transition_ref[:, 0:128] * row[:, 0:128]
        for block in range(128, width, 128):
            moved += transition_ref[:, block : block + 128] * row[:, block : block + 128]
        moved += jnp.where(lanes == 2 * at, drive_columns_ref[...], 0.0)
        column = jnp.broadcast_to(jnp.sum(moved, axis=1, keepdims=True), (width, 128))
        column *= factors_ref[at]
        row = jnp.concatenate(
            [
                jnp.sum(moved_ref[:, block : block + 128] * column, axis=0, keepdims=True)
                for block in range(0, width, 128)
            ],
            axis=1,
        )
        row += drive_ref[pl.ds(2 * at + 1, 1), :]
        return row * scale_ref[pl.ds(2 * at + 1, 1), :]

    def recorded(at, row):
        between_ref[pl.ds(2 * at, 1), :] = row
        row = two_steps(at, row)
        states_ref[pl.ds(2 * at + 1, 1), :] = row
        return row

    def owner(at):
        step = start + at * PIECE
        window = step // STEP_DEV
        return window % n_seg, window // n_seg, step % STEP_DEV

    def piece_copies(at):
        to_seg, to_grp, row = owner(at)
        own = jnp.logical_and(to_seg == seg, to_grp == grp)
        source = states_ref.at[pl.ds(pl.multiple_of(at * PIECE, PIECE), PIECE)]
        target = final_ref.at[pl.ds(pl.multiple_of(row, PIECE), PIECE)]
        remote = pltpu.make_async_remote_copy(
            src_ref=source,
            dst_ref=target,
            send_sem=piece_sems.at[at],
            recv_sem=final_sem,
            device_id={"seg": to_seg, "grp": to_grp},
        )
        return own, pltpu.make_async_copy(source, target, final_sem), remote

    @pl.when(core == 1)
    def _():
        @pl.when(is_middle)
        def _():
            start_maps(PARTS[1], False)
            map_groups(PARTS[1], 1, groups, False)
            share_copy().wait_recv()
            shift_copy().wait_recv()

        @pl.when(q > 0)
        def _():
            landed(into_ref, into_sem)

        @pl.when(is_middle)
        def _():
            send_ref[...] = row_times(into_ref[...], map_ref) + shift_in_ref[...]
            copies = chain_copies(q + 1)
            for copy in copies:
                copy.start()
            for copy in copies:
                copy.wait_send()

        for copy in mate_copies():
            copy.wait_send()

    @pl.when(core == 0)
    def _():
        start_maps(PARTS[0], True)
        map_groups(PARTS[0], 1, 1 + BEFORE_LINE, True)
        landed(plane_in_ref, plane_sems.at[1])
        plane_sum_ref[0:COLUMN] += jnp.sum(plane_in_ref[...], axis=0)

        def column_rows(z):
            begin = pl.multiple_of(lay.column_start(z, spot), 8)
            return pl.ds(begin, LEAST[z] + EXTRA)

        def line_copy(z):
            at = (z - level + DEPTH - 1) % DEPTH
            return pltpu.make_async_remote_copy(
                src_ref=plane_sum_ref.at[column_rows(z)],
                dst_ref=line_in_ref.at[at, 0 : LEAST[z] + EXTRA],
                send_sem=line_send_sems.at[z],
                recv_sem=line_sem,
                device_id=lay.device(z, spot, 0),
            )

        for z in range(DEPTH):

            @pl.when(level != z)
            def _():
                line_copy(z).start()

        map_groups(PARTS[0], 1 + BEFORE_LINE, 1 + TABLED, True)
        tabulate(LONGEST // 2 - 1)

        @pl.when(is_middle)
        def _():
            map_groups(PARTS[0], 1 + TABLED, groups, False)
            share_copy().start()

        for z in range(DEPTH):

            @pl.when(level == z)
            def _():
                most = LEAST[z] + EXTRA
                coming = line_in_ref.at[:, 0:most]
                landed(coming, line_sem)
                sums = plane_sum_ref[column_rows(z), :] + jnp.sum(coming[...], axis=0)
                drive_ref[0:most, :] = gains_ref[...] * sums
                if most < LONGEST:
                    drive_ref[most:, :] = jnp.zeros((LONGEST - most, width), F32)

        filler = jnp.zeros((128 - LONGEST, width), F32)
        drive_columns_ref[...] = jnp.transpose(jnp.concatenate([drive_ref[...], filler], axis=0))

        @pl.when(is_middle)
        def _():
            shift_ref[...] = lax.fori_loop(0, length // 2, two_steps, jnp.zeros_like(initial_ref))
            shift_copy().start()

        between_ref[...] = jnp.zeros_like(between_ref)
        states_ref[...] = jnp.zeros_like(states_ref)

        @pl.when(q == 0)
        def _():
            into_ref[...] = initial_ref[...]

        @pl.when(q > 0)
        def _():
            landed(into_ref, into_sem)

        last = lax.fori_loop(0, length // 2, recorded, into_ref[...])

        @pl.when(q == 0)
        def _():
            send_ref[...] = last
            for copy in chain_copies(1):
                copy.start()

        before = between_ref[...]
        upper, lower = split(before)
        moved = product(upper, lower, upper_ref[...], lower_ref[...]) + before * diagonal
        between = (moved + drive_ref[...]) * scale_ref[...]
        parity = lax.broadcasted_iota(jnp.int32, (LONGEST, width), 0) % 2
        states_ref[...] = jnp.where(parity == 0, between, states_ref[...])

        def send_piece(at, carry):
            own, local, remote = piece_copies(at)

            @pl.when(own)
            def _():
                local.start()

            @pl.when(jnp.logical_not(own))
            def _():
                remote.start()

            return carry

        lax.fori_loop(0, length // PIECE, send_piece, 0)

        @pl.when(q == 0)
        def _():
            for copy in chain_copies(1):
                copy.wait_send()

        @pl.when(is_middle)
        def _():
            share_copy().wait_send()
            shift_copy().wait_send()

        for z in range(DEPTH):

            @pl.when(level != z)
            def _():
                line_copy(z).wait_send()

        landed(plane_out_ref, plane_sems.at[0])

    landed(final_ref, final_sem)
    out_ref[...] = final_ref[...]

    @pl.when(core == 0)
    def _():
        def sent_piece(at, carry):
            own, _, remote = piece_copies(at)

            @pl.when(jnp.logical_not(own))
            def _():
                remote.wait_send()

            return carry

        lax.fori_loop(0, length // PIECE, sent_piece, 0)

    landed(counts_in_ref, counts_sems.at[0])


def filtered(lay, initial, transition, moved, gains, counts, where_step, tiles):
    n_dev, n_plane = lay.n_seg * lay.n_grp, lay.n_plane
    tile_count, width = tiles.shape
    row = pltpu.VMEM((1, width), F32)
    dma = pltpu.SemaphoreType.DMA
    return pl.pallas_call(
        functools.partial(filter_kernel, lay),
        out_shape=jax.ShapeDtypeStruct((STEP_DEV, width), F32),
        in_specs=[VMEM] * 7,
        out_specs=VMEM,
        scratch_shapes=[
            pltpu.VMEM((width, width), BF16),
            pltpu.VMEM((width, width), BF16),
            pltpu.VMEM((width, width), F32),
            pltpu.VMEM((LONGEST, width), F32),
            pltpu.VMEM((LONGEST, 128), F32),
            pltpu.VMEM((width, 128), F32),
            pltpu.VMEM((LONGEST // 2, width, 128), F32),
            pltpu.VMEM((LONGEST, width), F32),
            pltpu.VMEM((width, 128), F32),
            pltpu.VMEM((LONGEST, width), F32),
            pltpu.VMEM((LONGEST, width), F32),
            pltpu.VMEM((STEP_DEV, width), F32),
            pltpu.VMEM((tile_count, width), F32),
            pltpu.VMEM((1, tile_count), jnp.int32),
            pltpu.VMEM((2 * tile_count, width), BF16),
            pltpu.VMEM((2 * tile_count, width), BF16),
            pltpu.VMEM((n_dev - 1, 1, 128), F32),
            pltpu.VMEM((n_plane - 1, COLUMN, width), F32),
            pltpu.VMEM((n_plane - 1, COLUMN, width), F32),
            pltpu.VMEM((COLUMN + EXTRA, width), F32),
            pltpu.VMEM((DEPTH - 1, LONGEST, width), F32),
            row,
            row,
            row,
            row,
            dma((2,)),
            dma((4,)),
            dma((2,)),
            dma((DEPTH,)),
            dma,
            dma((2,)),
            dma((2,)),
            dma,
            dma((2,)),
            dma((LONGEST // PIECE,)),
            dma,
        ],
        compiler_params=pltpu.CompilerParams(
            collective_id=0, has_side_effects=True, vmem_limit_bytes=52 << 20
        ),
    )(initial, transition, moved, gains, counts, where_step, tiles)


def on_device(initial_state, transition, gains, tiles, tile_owner, tile_step):
    lay = Layout(lax.axis_size("seg"), lax.axis_size("grp"))
    where_step = tile_owner[0, :, 0] * STEP_DEV + tile_step[0]
    bins = np.full((lay.n_chip, 128), -1, np.int32)
    for q in range(lay.n_chip):
        level, at = q // lay.n_plane, q % lay.n_plane
        length = lay.length(level, at)
        bins[q, :length] = lay.first_step(level, at) + np.arange(length)
    counts = jnp.sum((jnp.asarray(bins)[:, :, None] == where_step[None, None, :]).astype(F32), axis=2)
    states = filtered(
        lay,
        initial_state[None],
        transition,
        transition.T,
        gains[None],
        counts[:, None, :],
        where_step[None],
        tiles[0],
    )
    return states[None]


def solution(mesh):
    in_specs = (P(), P(), P(), P("grp", "seg", None), P("grp", "seg", None), P("grp", "seg"))
    out_specs = P("grp", "seg", None)
    return jax.shard_map(
        on_device, mesh=mesh, in_specs=in_specs, out_specs=out_specs, check_vma=False
    )
```

```python
import functools

import jax
import jax.numpy as jnp
from jax import lax
from jax.experimental import pallas as pl
from jax.experimental.pallas import tpu as pltpu
from jax.sharding import PartitionSpec as P

STEP_DEV = 32
LENGTHS = ((64, 32, 40, 48), (56, 56, 56, 64), (72, 72, 72, 80), (80, 80, 80, 72))
FLAT = sum(LENGTHS, ())
BLOCKS = len(LENGTHS[0])
MOST = tuple(max(lengths) for lengths in LENGTHS)
DEPTH = len(LENGTHS)
LONGEST = max(MOST)
PIECE = 8
PARTS = ((0, 112), (112, 208)), ((208, 368), (368, 512))
SHARE = PARTS[0][-1][1]
FIRST = 7

F32 = jnp.float32
BF16 = jnp.bfloat16
VMEM = pl.BlockSpec(memory_space=pltpu.VMEM)


class Layout:
    def __init__(self, n_seg, n_grp):
        self.n_seg, self.n_grp = n_seg, n_grp
        self.n_chip = n_seg * n_grp // 2
        self.n_plane = self.n_chip // DEPTH
        self.core_in_seg = n_seg // DEPTH > n_grp
        self.n_x = n_seg // DEPTH // (2 if self.core_in_seg else 1)

    def turn(self, level, at):
        return at + (self.n_plane - 1 - 2 * at) * (level % 2)

    def device(self, level, spot, core):
        y, x = spot // self.n_x, spot % self.n_x
        x = self.n_x - 1 - x - (self.n_x - 1 - 2 * x) * (y % 2)
        y = self.n_plane // self.n_x - 1 - y
        if self.core_in_seg:
            return {"seg": (level * self.n_x + x) * 2 + core, "grp": y}
        return {"seg": level * self.n_x + x, "grp": y * 2 + core}

    def chip(self, q, core):
        level = q // self.n_plane
        return self.device(level, self.turn(level, q % self.n_plane), core)

    def here(self, seg, grp):
        if self.core_in_seg:
            core, y, across = seg % 2, grp, seg // 2
        else:
            core, y, across = grp % 2, grp // 2, seg
        level, x = across // self.n_x, across % self.n_x
        y = self.n_plane // self.n_x - 1 - y
        x = self.n_x - 1 - x
        x = x + (self.n_x - 1 - 2 * x) * (y % 2)
        return level, y * self.n_x + x, core

    def block(self, q):
        return q * BLOCKS // self.n_plane

    def length(self, q):
        return pick(FLAT, self.block(q))

    def first_step(self, q):
        some = self.n_plane // BLOCKS
        starts = [sum(FLAT[:at]) * some for at in range(len(FLAT))]
        block = self.block(q)
        return pick(starts, block) + (q - block * some) * pick(FLAT, block)

    def index(self, level, spot):
        return level * self.n_plane + self.turn(level, spot)


def pick(table, index):
    if isinstance(index, int):
        return table[index]
    return table[0] + sum((table[at] - table[0]) * (index == at).astype(jnp.int32) for at in range(1, len(table)))


def split(value):
    upper = value.astype(BF16)
    return upper, (value - upper.astype(F32)).astype(BF16)


def product(upper, lower, right_upper, right_lower):
    dot = functools.partial(jnp.dot, preferred_element_type=F32)
    return dot(upper, right_upper) + dot(lower, right_upper) + dot(upper, right_lower)


def stacked_product(upper, lower, right_upper, right_lower):
    dot = functools.partial(jnp.dot, preferred_element_type=F32)
    both = dot(jnp.concatenate([upper, lower], axis=0), right_upper)
    rows = upper.shape[0]
    return both[:rows] + both[rows:] + dot(upper, right_lower)


def row_times(row, matrix_ref):
    depth, width = matrix_ref.shape
    column = jnp.transpose(jnp.broadcast_to(row, (128, depth)))
    return jnp.concatenate(
        [
            jnp.sum(matrix_ref[:, at : at + 128] * column, axis=0, keepdims=True)
            for at in range(0, width, 128)
        ],
        axis=1,
    )


def filter_kernel(
    lay,
    initial_ref,
    transition_ref,
    gains_ref,
    where_ref,
    tiles_ref,
    out_ref,
    moved_ref,
    counts_ref,
    upper_ref,
    lower_ref,
    map_ref,
    scale_ref,
    column_ref,
    gains_column_ref,
    factors_ref,
    drive_ref,
    drive_columns_ref,
    between_ref,
    states_ref,
    final_ref,
    mate_tiles_ref,
    mate_where_ref,
    tile_upper_ref,
    tile_lower_ref,
    counts_in_ref,
    plane_out_ref,
    plane_in_ref,
    plane_sum_ref,
    line_in_ref,
    into_ref,
    send_ref,
    shift_ref,
    shift_in_ref,
    counts_sems,
    mate_sems,
    plane_send_sems,
    plane_sems,
    line_send_sems,
    line_sem,
    share_sems,
    shift_sems,
    into_sem,
    send_sems,
    piece_sems,
    final_sem,
):
    n_seg, n_grp = lay.n_seg, lay.n_grp
    n_dev, n_plane, n_chip = n_seg * n_grp, lay.n_plane, lay.n_chip
    seg, grp = lax.axis_index("seg"), lax.axis_index("grp")
    level, spot, core = lay.here(seg, grp)
    at_level = lay.turn(level, spot)
    q = level * n_plane + at_level
    me = q * 2 + core
    length = lay.length(q)
    start = lay.first_step(q)
    groups = length // 8
    width = map_ref.shape[1]
    tile_count = tiles_ref.shape[0]
    barrier = pltpu.get_barrier_semaphore()

    def greet(at, carry):
        other = (me + 1 + at) % n_dev
        pl.semaphore_signal(barrier, inc=1, device_id=lay.chip(other // 2, other % 2))
        return carry

    lax.fori_loop(0, n_dev - 1, greet, 0)

    where_columns = jnp.transpose(jnp.broadcast_to(where_ref[...].astype(F32), (128, tile_count)))
    bins = lax.broadcasted_iota(jnp.int32, (1, 128), 1)

    def count(at, carry):
        steps = jnp.where(bins < lay.length(at), bins + lay.first_step(at), -1).astype(F32)
        counts_ref[at] = jnp.sum((where_columns == steps).astype(F32), axis=0, keepdims=True)
        return carry

    lax.fori_loop(0, n_chip, count, 0)
    pl.semaphore_wait(barrier, n_dev - 1)

    def landed(ref, sem):
        pltpu.make_async_copy(ref, ref, sem).wait()

    def mate_copies():
        return [
            pltpu.make_async_remote_copy(
                src_ref=source,
                dst_ref=target,
                send_sem=mate_sems.at[2 * at],
                recv_sem=mate_sems.at[2 * at + 1],
                device_id=lay.device(level, spot, 0),
            )
            for at, (source, target) in enumerate(
                ((tiles_ref, mate_tiles_ref), (where_ref, mate_where_ref))
            )
        ]

    @pl.when(core == 1)
    def _():
        for copy in mate_copies():
            copy.start()

    def send_counts(at, carry):
        other = (me + 1 + at) % n_dev
        pltpu.make_async_remote_copy(
            src_ref=counts_ref.at[other // 2],
            dst_ref=counts_in_ref.at[at],
            send_sem=counts_sems.at[0],
            recv_sem=counts_sems.at[1],
            device_id=lay.chip(other // 2, other % 2),
        ).start()
        return carry

    lax.fori_loop(0, n_dev - 1, send_counts, 0)

    moved_ref[...] = jnp.transpose(transition_ref[...])
    row_ids = lax.broadcasted_iota(jnp.int32, (width, width), 0)
    column_ids = lax.broadcasted_iota(jnp.int32, (width, width), 1)
    on_diagonal = row_ids == column_ids
    diagonal = jnp.sum(jnp.where(on_diagonal, moved_ref[...], 0.0), axis=0, keepdims=True)
    upper, lower = split(jnp.where(on_diagonal, 0.0, moved_ref[...]))
    upper_ref[...] = upper
    lower_ref[...] = lower

    def plane_copy(z, spot_to):
        at = (spot_to - spot + n_plane - 1) % n_plane
        return pltpu.make_async_remote_copy(
            src_ref=plane_out_ref.at[z, at, 0 : MOST[z]],
            dst_ref=plane_in_ref.at[z, at, 0 : MOST[z]],
            send_sem=plane_send_sems.at[z],
            recv_sem=plane_sems.at[z],
            device_id=lay.device(level, spot_to, 0),
        )

    def bin_level(z):
        where = jnp.concatenate([where_ref[...], mate_where_ref[...]], axis=1)
        rows = lax.broadcasted_iota(jnp.int32, (MOST[z], 1), 0)
        dot = functools.partial(jnp.dot, preferred_element_type=F32)

        def some(group, carry):
            columns = [group * BLOCKS + ahead for ahead in range(BLOCKS)]
            placed = [
                (rows + lay.first_step(lay.index(z, column)) == where).astype(F32)
                for column in columns
            ]
            placed = jnp.concatenate(placed, axis=0).astype(BF16)
            sums = dot(placed, tile_upper_ref[...]) + dot(placed, tile_lower_ref[...])
            for ahead, column in enumerate(columns):
                part = sums[ahead * MOST[z] : (ahead + 1) * MOST[z]]

                @pl.when(column == spot)
                def _():
                    plane_sum_ref[z, 0 : MOST[z]] = part

                @pl.when(column != spot)
                def _():
                    at = (column - spot + n_plane - 1) % n_plane
                    plane_out_ref[z, at, 0 : MOST[z]] = part
                    plane_copy(z, column).start()

            return carry

        lax.fori_loop(0, n_plane // BLOCKS, some, 0)

    @pl.when(core == 0)
    def _():
        upper, lower = split(tiles_ref[...])
        tile_upper_ref[0:tile_count] = upper
        tile_lower_ref[0:tile_count] = lower
        for copy in mate_copies():
            copy.wait_recv()
        upper, lower = split(mate_tiles_ref[...])
        tile_upper_ref[tile_count:] = upper
        tile_lower_ref[tile_count:] = lower
        bin_level(0)
        bin_level(1)
        gains_column_ref[...] = jnp.transpose(jnp.broadcast_to(gains_ref[...], (128, width)))

    landed(counts_in_ref, counts_sems.at[1])
    counts = counts_ref[q] + jnp.sum(counts_in_ref[...], axis=0)
    column = jnp.transpose(jnp.broadcast_to(counts, (128, 128)))[:LONGEST]
    for at in range(0, width, 128):
        scale_ref[:, at : at + 128] = 1.0 / (1.0 + column * gains_ref[:, at : at + 128])
    column_ref[...] = column

    def tabulate(entry):
        count = column_ref[pl.ds(2 * entry, 1), :]
        whole = 1.0 + count * gains_column_ref[...]
        near = pl.reciprocal(whole, approx=True)
        near = near * (2.0 - whole * near)
        factors_ref[entry] = near * (2.0 - whole * near)

    def advance_maps(parts, first, count, tabled):
        values = [map_ref[begin:end, :] for begin, end in parts]
        for ahead in range(count):
            factor = scale_ref[pl.ds(first + ahead, 1), :]
            for at, value in enumerate(values):
                upper, lower = split(value)
                multiply = stacked_product if parts is PARTS[0] else product
                joined = multiply(upper, lower, upper_ref[...], lower_ref[...])
                values[at] = (joined + value * diagonal) * factor
            if tabled:
                tabulate(first + ahead - 1)
        for (begin, end), value in zip(parts, values):
            map_ref[begin:end, :] = value

    def start_maps(parts, tabled):
        for begin, end in parts:
            map_ref[begin:end, :] = moved_ref[begin:end, :] * scale_ref[pl.ds(0, 1), :]
        advance_maps(parts, 1, FIRST, tabled)

    def map_groups(parts, begin, end, tabled):
        def group(at, carry):
            advance_maps(parts, 8 * at, 8, tabled)
            return carry

        lax.fori_loop(begin, end, group, 0)

    is_middle = jnp.logical_and(q > 0, q < n_chip - 1)

    def chain_copies(q_next):
        return [
            pltpu.make_async_remote_copy(
                src_ref=send_ref,
                dst_ref=into_ref,
                send_sem=send_sems.at[other],
                recv_sem=into_sem,
                device_id=lay.chip(q_next, other),
            )
            for other in (1, 0)
        ]

    share_ref = map_ref.at[0:SHARE]

    def share_copy():
        return pltpu.make_async_remote_copy(
            src_ref=share_ref,
            dst_ref=share_ref,
            send_sem=share_sems.at[0],
            recv_sem=share_sems.at[1],
            device_id=lay.device(level, spot, 1),
        )

    def shift_copy():
        return pltpu.make_async_remote_copy(
            src_ref=shift_ref,
            dst_ref=shift_in_ref,
            send_sem=shift_sems.at[0],
            recv_sem=shift_sems.at[1],
            device_id=lay.device(level, spot, 1),
        )

    lanes = lax.broadcasted_iota(jnp.int32, (width, 128), 1)

    def two_steps(at, row):
        moved = transition_ref[:, 0:128] * row[:, 0:128]
        for block in range(128, width, 128):
            moved += transition_ref[:, block : block + 128] * row[:, block : block + 128]
        moved += jnp.where(lanes == 2 * at, drive_columns_ref[...], 0.0)
        column = jnp.broadcast_to(jnp.sum(moved, axis=1, keepdims=True), (width, 128))
        column *= factors_ref[at]
        row = jnp.concatenate(
            [
                jnp.sum(moved_ref[:, block : block + 128] * column, axis=0, keepdims=True)
                for block in range(0, width, 128)
            ],
            axis=1,
        )
        row += drive_ref[pl.ds(2 * at + 1, 1), :]
        return row * scale_ref[pl.ds(2 * at + 1, 1), :]

    def recorded(at, row):
        between_ref[pl.ds(2 * at, 1), :] = row
        row = two_steps(at, row)
        states_ref[pl.ds(2 * at + 1, 1), :] = row
        return row

    def owner(at):
        step = start + at * PIECE
        window = step // STEP_DEV
        return window % n_seg, window // n_seg, step % STEP_DEV

    def piece_copies(at):
        to_seg, to_grp, row = owner(at)
        own = jnp.logical_and(to_seg == seg, to_grp == grp)
        source = states_ref.at[pl.ds(pl.multiple_of(at * PIECE, PIECE), PIECE)]
        target = final_ref.at[pl.ds(pl.multiple_of(row, PIECE), PIECE)]
        remote = pltpu.make_async_remote_copy(
            src_ref=source,
            dst_ref=target,
            send_sem=piece_sems.at[at],
            recv_sem=final_sem,
            device_id={"seg": to_seg, "grp": to_grp},
        )
        return own, pltpu.make_async_copy(source, target, final_sem), remote

    @pl.when(core == 1)
    def _():
        @pl.when(is_middle)
        def _():
            start_maps(PARTS[1], False)
            map_groups(PARTS[1], 1, groups, False)
            share_copy().wait_recv()
            shift_copy().wait_recv()

        @pl.when(q > 0)
        def _():
            landed(into_ref, into_sem)

        @pl.when(is_middle)
        def _():
            send_ref[...] = row_times(into_ref[...], map_ref) + shift_in_ref[...]
            copies = chain_copies(q + 1)
            for copy in copies:
                copy.start()
            for copy in copies:
                copy.wait_send()

        for copy in mate_copies():
            copy.wait_send()

    @pl.when(core == 0)
    def _():
        def sum_level(z):
            rows = pl.ds(0, MOST[z])
            landed(plane_in_ref.at[z, :, rows], plane_sems.at[z])
            plane_sum_ref[z, rows] += jnp.sum(plane_in_ref[z, :, rows], axis=0)

            @pl.when(level != z)
            def _():
                line_copy(z).start()

        def line_copy(z):
            at = (z - level + DEPTH - 1) % DEPTH
            return pltpu.make_async_remote_copy(
                src_ref=plane_sum_ref.at[z, 0 : MOST[z]],
                dst_ref=line_in_ref.at[at, 0 : MOST[z]],
                send_sem=line_send_sems.at[z],
                recv_sem=line_sem,
                device_id=lay.device(z, spot, 0),
            )

        def take_level(z):
            coming = line_in_ref.at[:, 0 : MOST[z]]
            landed(coming, line_sem)
            sums = plane_sum_ref[z, 0 : MOST[z]] + jnp.sum(coming[...], axis=0)
            drive_ref[0 : MOST[z], :] = gains_ref[...] * sums
            filler = jnp.zeros((128 - LONGEST, width), F32)
            drive_columns_ref[...] = jnp.transpose(
                jnp.concatenate([drive_ref[...], filler], axis=0)
            )

        def tabulate_all():
            def entry(at, carry):
                tabulate(at)
                return carry

            lax.fori_loop(0, LONGEST // 2, entry, 0)

        def scan_into(row):
            return lax.fori_loop(0, length // 2, recorded, row)

        drive_ref[...] = jnp.zeros_like(drive_ref)
        between_ref[...] = jnp.zeros_like(between_ref)
        states_ref[...] = jnp.zeros_like(states_ref)

        @pl.when(q == 0)
        def _():
            for z in range(2, DEPTH):
                bin_level(z)
            tabulate_all()
            sum_level(0)
            take_level(0)
            send_ref[...] = scan_into(initial_ref[...])
            for copy in chain_copies(1):
                copy.start()
            for z in range(1, DEPTH):
                sum_level(z)
            for copy in chain_copies(1):
                copy.wait_send()

        @pl.when(is_middle)
        def _():
            start_maps(PARTS[0], True)
            for z in range(DEPTH):
                if z + 2 < DEPTH:
                    bin_level(z + 2)
                sum_level(z)
                map_groups(PARTS[0], 1 + z, jnp.minimum(2 + z, groups), True)
            map_groups(PARTS[0], 1 + DEPTH, groups, False)
            share_copy().start()
            tabulate(LONGEST // 2 - 1)

        @pl.when(q == n_chip - 1)
        def _():
            for z in range(DEPTH):
                if z + 2 < DEPTH:
                    bin_level(z + 2)
                sum_level(z)
            tabulate_all()

        for z in range(DEPTH):

            @pl.when(jnp.logical_and(level == z, q > 0))
            def _():
                take_level(z)

        @pl.when(is_middle)
        def _():
            shift_ref[...] = lax.fori_loop(0, length // 2, two_steps, jnp.zeros_like(initial_ref))
            shift_copy().start()

        @pl.when(q > 0)
        def _():
            landed(into_ref, into_sem)
            scan_into(into_ref[...])

        before = between_ref[...]
        upper, lower = split(before)
        moved = product(upper, lower, upper_ref[...], lower_ref[...]) + before * diagonal
        between = (moved + drive_ref[...]) * scale_ref[...]
        parity = lax.broadcasted_iota(jnp.int32, (LONGEST, width), 0) % 2
        states_ref[...] = jnp.where(parity == 0, between, states_ref[...])

        def send_piece(at, carry):
            own, local, remote = piece_copies(at)

            @pl.when(own)
            def _():
                local.start()

            @pl.when(jnp.logical_not(own))
            def _():
                remote.start()

            return carry

        lax.fori_loop(0, length // PIECE, send_piece, 0)

        @pl.when(is_middle)
        def _():
            share_copy().wait_send()
            shift_copy().wait_send()

        for z in range(DEPTH):

            @pl.when(level != z)
            def _():
                line_copy(z).wait_send()

        for z in range(DEPTH):
            landed(plane_out_ref.at[z, :, 0 : MOST[z]], plane_send_sems.at[z])

    landed(final_ref, final_sem)
    out_ref[...] = final_ref[...]

    @pl.when(core == 0)
    def _():
        def sent_piece(at, carry):
            own, _, remote = piece_copies(at)

            @pl.when(jnp.logical_not(own))
            def _():
                remote.wait_send()

            return carry

        lax.fori_loop(0, length // PIECE, sent_piece, 0)

    landed(counts_in_ref, counts_sems.at[0])


def filtered(lay, initial, transition, gains, where_step, tiles):
    n_dev, n_plane = lay.n_seg * lay.n_grp, lay.n_plane
    tile_count, width = tiles.shape
    row = pltpu.VMEM((1, width), F32)
    dma = pltpu.SemaphoreType.DMA
    return pl.pallas_call(
        functools.partial(filter_kernel, lay),
        out_shape=jax.ShapeDtypeStruct((STEP_DEV, width), F32),
        in_specs=[VMEM] * 5,
        out_specs=VMEM,
        scratch_shapes=[
            pltpu.VMEM((width, width), F32),
            pltpu.VMEM((lay.n_chip, 1, 128), F32),
            pltpu.VMEM((width, width), BF16),
            pltpu.VMEM((width, width), BF16),
            pltpu.VMEM((width, width), F32),
            pltpu.VMEM((LONGEST, width), F32),
            pltpu.VMEM((LONGEST, 128), F32),
            pltpu.VMEM((width, 128), F32),
            pltpu.VMEM((LONGEST // 2, width, 128), F32),
            pltpu.VMEM((LONGEST, width), F32),
            pltpu.VMEM((width, 128), F32),
            pltpu.VMEM((LONGEST, width), F32),
            pltpu.VMEM((LONGEST, width), F32),
            pltpu.VMEM((STEP_DEV, width), F32),
            pltpu.VMEM((tile_count, width), F32),
            pltpu.VMEM((1, tile_count), jnp.int32),
            pltpu.VMEM((2 * tile_count, width), BF16),
            pltpu.VMEM((2 * tile_count, width), BF16),
            pltpu.VMEM((n_dev - 1, 1, 128), F32),
            pltpu.VMEM((DEPTH, n_plane - 1, LONGEST, width), F32),
            pltpu.VMEM((DEPTH, n_plane - 1, LONGEST, width), F32),
            pltpu.VMEM((DEPTH, LONGEST, width), F32),
            pltpu.VMEM((DEPTH - 1, LONGEST, width), F32),
            row,
            row,
            row,
            row,
            dma((2,)),
            dma((4,)),
            dma((DEPTH,)),
            dma((DEPTH,)),
            dma((DEPTH,)),
            dma,
            dma((2,)),
            dma((2,)),
            dma,
            dma((2,)),
            dma((LONGEST // PIECE,)),
            dma,
        ],
        compiler_params=pltpu.CompilerParams(
            collective_id=0, has_side_effects=True, vmem_limit_bytes=52 << 20
        ),
    )(initial, transition, gains, where_step, tiles)


def on_device(initial_state, transition, gains, tiles, tile_owner, tile_step):
    lay = Layout(lax.axis_size("seg"), lax.axis_size("grp"))
    where_step = tile_owner[0, :, 0] * STEP_DEV + tile_step[0]
    states = filtered(
        lay,
        initial_state[None],
        transition,
        gains[None],
        where_step[None],
        tiles[0],
    )
    return states[None]


def solution(mesh):
    in_specs = (P(), P(), P(), P("grp", "seg", None), P("grp", "seg", None), P("grp", "seg"))
    out_specs = P("grp", "seg", None)
    return jax.shard_map(
        on_device, mesh=mesh, in_specs=in_specs, out_specs=out_specs, check_vma=False
    )
```

```python
import functools

import jax
import jax.numpy as jnp
from jax import lax
from jax.experimental import pallas as pl
from jax.experimental.pallas import tpu as pltpu
from jax.sharding import PartitionSpec as P

STEP_DEV = 32
LENGTHS = ((88, 40, 40, 48), (48, 56, 56, 56), (64, 64, 72, 72), (80, 80, 80, 80))
FLAT = sum(LENGTHS, ())
BLOCKS = len(LENGTHS[0])
MOST = tuple(max(lengths) for lengths in LENGTHS)
DEPTH = len(LENGTHS)
LONGEST = max(MOST)
PIECE = 8
PARTS = ((0, 112), (112, 208)), ((208, 368), (368, 512))
SHARE = PARTS[0][-1][1]
FIRST = 7

F32 = jnp.float32
BF16 = jnp.bfloat16
VMEM = pl.BlockSpec(memory_space=pltpu.VMEM)
HBM = pl.BlockSpec(memory_space=pltpu.HBM)


class Layout:
    def __init__(self, n_seg, n_grp):
        self.n_seg, self.n_grp = n_seg, n_grp
        self.n_chip = n_seg * n_grp // 2
        self.n_plane = self.n_chip // DEPTH
        self.core_in_seg = n_seg // DEPTH > n_grp
        self.n_x = n_seg // DEPTH // (2 if self.core_in_seg else 1)

    def turn(self, level, at):
        return at + (self.n_plane - 1 - 2 * at) * (level % 2)

    def device(self, level, spot, core):
        y, x = spot // self.n_x, spot % self.n_x
        x = self.n_x - 1 - x - (self.n_x - 1 - 2 * x) * (y % 2)
        y = self.n_plane // self.n_x - 1 - y
        if self.core_in_seg:
            return {"seg": (level * self.n_x + x) * 2 + core, "grp": y}
        return {"seg": level * self.n_x + x, "grp": y * 2 + core}

    def chip(self, q, core):
        level = q // self.n_plane
        return self.device(level, self.turn(level, q % self.n_plane), core)

    def here(self, seg, grp):
        if self.core_in_seg:
            core, y, across = seg % 2, grp, seg // 2
        else:
            core, y, across = grp % 2, grp // 2, seg
        level, x = across // self.n_x, across % self.n_x
        y = self.n_plane // self.n_x - 1 - y
        x = self.n_x - 1 - x
        x = x + (self.n_x - 1 - 2 * x) * (y % 2)
        return level, y * self.n_x + x, core

    def block(self, q):
        return q * BLOCKS // self.n_plane

    def length(self, q):
        return pick(FLAT, self.block(q))

    def first_step(self, q):
        some = self.n_plane // BLOCKS
        starts = [sum(FLAT[:at]) * some for at in range(len(FLAT))]
        block = self.block(q)
        return pick(starts, block) + (q - block * some) * pick(FLAT, block)

    def index(self, level, spot):
        return level * self.n_plane + self.turn(level, spot)


def pick(table, index):
    if isinstance(index, int):
        return table[index]
    return table[0] + sum((table[at] - table[0]) * (index == at).astype(jnp.int32) for at in range(1, len(table)))


def split(value):
    upper = value.astype(BF16)
    return upper, (value - upper.astype(F32)).astype(BF16)


def product(upper, lower, right_upper, right_lower):
    dot = functools.partial(jnp.dot, preferred_element_type=F32)
    return dot(upper, right_upper) + dot(lower, right_upper) + dot(upper, right_lower)


def stacked_product(upper, lower, right_upper, right_lower):
    dot = functools.partial(jnp.dot, preferred_element_type=F32)
    both = dot(jnp.concatenate([upper, lower], axis=0), right_upper)
    rows = upper.shape[0]
    return both[:rows] + both[rows:] + dot(upper, right_lower)


def row_times(row, matrix_ref):
    depth, width = matrix_ref.shape
    column = jnp.transpose(jnp.broadcast_to(row, (128, depth)))
    return jnp.concatenate(
        [
            jnp.sum(matrix_ref[:, at : at + 128] * column, axis=0, keepdims=True)
            for at in range(0, width, 128)
        ],
        axis=1,
    )


def filter_kernel(
    lay,
    initial_hbm_ref,
    transition_hbm_ref,
    gains_hbm_ref,
    owner_hbm_ref,
    step_hbm_ref,
    tiles_hbm_ref,
    out_ref,
    initial_ref,
    transition_ref,
    gains_ref,
    owner_ref,
    step_ref,
    where_ref,
    tiles_ref,
    load_sems,
    moved_ref,
    counts_ref,
    upper_ref,
    lower_ref,
    map_ref,
    scale_ref,
    column_ref,
    gains_column_ref,
    factors_ref,
    drive_ref,
    drive_columns_ref,
    between_ref,
    states_ref,
    final_ref,
    mate_tiles_ref,
    mate_where_ref,
    tile_upper_ref,
    tile_lower_ref,
    counts_in_ref,
    plane_out_ref,
    plane_in_ref,
    plane_sum_ref,
    line_in_ref,
    into_ref,
    send_ref,
    shift_ref,
    shift_in_ref,
    counts_sems,
    mate_sems,
    plane_send_sems,
    plane_sems,
    line_send_sems,
    line_sem,
    share_sems,
    shift_sems,
    into_sem,
    send_sems,
    piece_sems,
    final_sem,
):
    n_seg, n_grp = lay.n_seg, lay.n_grp
    n_dev, n_plane, n_chip = n_seg * n_grp, lay.n_plane, lay.n_chip
    seg, grp = lax.axis_index("seg"), lax.axis_index("grp")
    level, spot, core = lay.here(seg, grp)
    at_level = lay.turn(level, spot)
    q = level * n_plane + at_level
    me = q * 2 + core
    length = lay.length(q)
    start = lay.first_step(q)
    groups = length // 8
    width = map_ref.shape[1]
    tile_count = tiles_ref.shape[0]
    barrier = pltpu.get_barrier_semaphore()

    def greet(at, carry):
        other = (me + 1 + at) % n_dev
        pl.semaphore_signal(barrier, inc=1, device_id=lay.chip(other // 2, other % 2))
        return carry

    loads = [
        pltpu.make_async_copy(source, target, load_sems.at[at])
        for at, (source, target) in enumerate(
            (
                (owner_hbm_ref, owner_ref),
                (step_hbm_ref, step_ref),
                (tiles_hbm_ref, tiles_ref),
                (transition_hbm_ref, transition_ref),
                (gains_hbm_ref, gains_ref),
                (initial_hbm_ref, initial_ref),
            )
        )
    ]
    for load in loads:
        load.start()
    lax.fori_loop(0, n_dev - 1, greet, 0)

    for load in loads[:2]:
        load.wait()
    where_ref[...] = owner_ref[...] * STEP_DEV + step_ref[...]
    where_columns = jnp.transpose(jnp.broadcast_to(where_ref[...].astype(F32), (128, tile_count)))
    bins = lax.broadcasted_iota(jnp.int32, (1, 128), 1)

    def count(at, carry):
        steps = jnp.where(bins < lay.length(at), bins + lay.first_step(at), -1).astype(F32)
        counts_ref[at] = jnp.sum((where_columns == steps).astype(F32), axis=0, keepdims=True)
        return carry

    lax.fori_loop(0, n_chip, count, 0)
    loads[2].wait()
    pl.semaphore_wait(barrier, n_dev - 1)

    def landed(ref, sem):
        pltpu.make_async_copy(ref, ref, sem).wait()

    def mate_copies():
        return [
            pltpu.make_async_remote_copy(
                src_ref=source,
                dst_ref=target,
                send_sem=mate_sems.at[2 * at],
                recv_sem=mate_sems.at[2 * at + 1],
                device_id=lay.device(level, spot, 0),
            )
            for at, (source, target) in enumerate(
                ((tiles_ref, mate_tiles_ref), (where_ref, mate_where_ref))
            )
        ]

    @pl.when(core == 1)
    def _():
        for copy in mate_copies():
            copy.start()

    def send_counts(at, carry):
        other = (me + 1 + at) % n_dev
        pltpu.make_async_remote_copy(
            src_ref=counts_ref.at[other // 2],
            dst_ref=counts_in_ref.at[at],
            send_sem=counts_sems.at[0],
            recv_sem=counts_sems.at[1],
            device_id=lay.chip(other // 2, other % 2),
        ).start()
        return carry

    lax.fori_loop(0, n_dev - 1, send_counts, 0)

    for load in loads[3:]:
        load.wait()
    moved_ref[...] = jnp.transpose(transition_ref[...])
    row_ids = lax.broadcasted_iota(jnp.int32, (width, width), 0)
    column_ids = lax.broadcasted_iota(jnp.int32, (width, width), 1)
    on_diagonal = row_ids == column_ids
    diagonal = jnp.sum(jnp.where(on_diagonal, moved_ref[...], 0.0), axis=0, keepdims=True)
    upper, lower = split(jnp.where(on_diagonal, 0.0, moved_ref[...]))
    upper_ref[...] = upper
    lower_ref[...] = lower

    def plane_copy(z, spot_to):
        at = (spot_to - spot + n_plane - 1) % n_plane
        return pltpu.make_async_remote_copy(
            src_ref=plane_out_ref.at[z, at, 0 : MOST[z]],
            dst_ref=plane_in_ref.at[z, at, 0 : MOST[z]],
            send_sem=plane_send_sems.at[z],
            recv_sem=plane_sems.at[z],
            device_id=lay.device(level, spot_to, 0),
        )

    def bin_level(z):
        where = jnp.concatenate([where_ref[...], mate_where_ref[...]], axis=1)
        rows = lax.broadcasted_iota(jnp.int32, (MOST[z], 1), 0)
        dot = functools.partial(jnp.dot, preferred_element_type=F32)

        def some(group, carry):
            columns = [group * BLOCKS + ahead for ahead in range(BLOCKS)]
            placed = [
                (rows + lay.first_step(lay.index(z, column)) == where).astype(F32)
                for column in columns
            ]
            placed = jnp.concatenate(placed, axis=0).astype(BF16)
            sums = dot(placed, tile_upper_ref[...]) + dot(placed, tile_lower_ref[...])
            for ahead, column in enumerate(columns):
                part = sums[ahead * MOST[z] : (ahead + 1) * MOST[z]]

                @pl.when(column == spot)
                def _():
                    plane_sum_ref[z, 0 : MOST[z]] = part

                @pl.when(column != spot)
                def _():
                    at = (column - spot + n_plane - 1) % n_plane
                    plane_out_ref[z, at, 0 : MOST[z]] = part
                    plane_copy(z, column).start()

            return carry

        lax.fori_loop(0, n_plane // BLOCKS, some, 0)

    @pl.when(core == 0)
    def _():
        upper, lower = split(tiles_ref[...])
        tile_upper_ref[0:tile_count] = upper
        tile_lower_ref[0:tile_count] = lower
        for copy in mate_copies():
            copy.wait_recv()
        upper, lower = split(mate_tiles_ref[...])
        tile_upper_ref[tile_count:] = upper
        tile_lower_ref[tile_count:] = lower
        bin_level(0)
        bin_level(1)
        gains_column_ref[...] = jnp.transpose(jnp.broadcast_to(gains_ref[...], (128, width)))

    landed(counts_in_ref, counts_sems.at[1])
    counts = counts_ref[q] + jnp.sum(counts_in_ref[...], axis=0)
    column = jnp.transpose(jnp.broadcast_to(counts, (128, 128)))[:LONGEST]
    for at in range(0, width, 128):
        scale_ref[:, at : at + 128] = 1.0 / (1.0 + column * gains_ref[:, at : at + 128])
    column_ref[...] = column

    def tabulate(entry):
        count = column_ref[pl.ds(2 * entry, 1), :]
        whole = 1.0 + count * gains_column_ref[...]
        near = pl.reciprocal(whole, approx=True)
        near = near * (2.0 - whole * near)
        factors_ref[entry] = near * (2.0 - whole * near)

    def advance_maps(parts, first, count, tabled):
        values = [map_ref[begin:end, :] for begin, end in parts]
        for ahead in range(count):
            factor = scale_ref[pl.ds(first + ahead, 1), :]
            for at, value in enumerate(values):
                upper, lower = split(value)
                multiply = stacked_product if parts is PARTS[0] else product
                joined = multiply(upper, lower, upper_ref[...], lower_ref[...])
                values[at] = (joined + value * diagonal) * factor
            if tabled:
                tabulate(first + ahead - 1)
        for (begin, end), value in zip(parts, values):
            map_ref[begin:end, :] = value

    def start_maps(parts, tabled):
        for begin, end in parts:
            map_ref[begin:end, :] = moved_ref[begin:end, :] * scale_ref[pl.ds(0, 1), :]
        advance_maps(parts, 1, FIRST, tabled)

    def map_groups(parts, begin, end, tabled):
        def group(at, carry):
            advance_maps(parts, 8 * at, 8, tabled)
            return carry

        lax.fori_loop(begin, end, group, 0)

    is_middle = jnp.logical_and(q > 0, q < n_chip - 1)

    def chain_copies(q_next):
        return [
            pltpu.make_async_remote_copy(
                src_ref=send_ref,
                dst_ref=into_ref,
                send_sem=send_sems.at[other],
                recv_sem=into_sem,
                device_id=lay.chip(q_next, other),
            )
            for other in (1, 0)
        ]

    share_ref = map_ref.at[0:SHARE]

    def share_copy():
        return pltpu.make_async_remote_copy(
            src_ref=share_ref,
            dst_ref=share_ref,
            send_sem=share_sems.at[0],
            recv_sem=share_sems.at[1],
            device_id=lay.device(level, spot, 1),
        )

    def shift_copy():
        return pltpu.make_async_remote_copy(
            src_ref=shift_ref,
            dst_ref=shift_in_ref,
            send_sem=shift_sems.at[0],
            recv_sem=shift_sems.at[1],
            device_id=lay.device(level, spot, 1),
        )

    lanes = lax.broadcasted_iota(jnp.int32, (width, 128), 1)

    def two_steps(at, row):
        moved = transition_ref[:, 0:128] * row[:, 0:128]
        for block in range(128, width, 128):
            moved += transition_ref[:, block : block + 128] * row[:, block : block + 128]
        moved += jnp.where(lanes == 2 * at, drive_columns_ref[...], 0.0)
        column = jnp.broadcast_to(jnp.sum(moved, axis=1, keepdims=True), (width, 128))
        column *= factors_ref[at]
        row = jnp.concatenate(
            [
                jnp.sum(moved_ref[:, block : block + 128] * column, axis=0, keepdims=True)
                for block in range(0, width, 128)
            ],
            axis=1,
        )
        row += drive_ref[pl.ds(2 * at + 1, 1), :]
        return row * scale_ref[pl.ds(2 * at + 1, 1), :]

    def recorded(at, row):
        between_ref[pl.ds(2 * at, 1), :] = row
        row = two_steps(at, row)
        states_ref[pl.ds(2 * at + 1, 1), :] = row
        return row

    def owner(at):
        step = start + at * PIECE
        window = step // STEP_DEV
        return window % n_seg, window // n_seg, step % STEP_DEV

    def piece_copies(at):
        to_seg, to_grp, row = owner(at)
        own = jnp.logical_and(to_seg == seg, to_grp == grp)
        source = states_ref.at[pl.ds(pl.multiple_of(at * PIECE, PIECE), PIECE)]
        target = final_ref.at[pl.ds(pl.multiple_of(row, PIECE), PIECE)]
        remote = pltpu.make_async_remote_copy(
            src_ref=source,
            dst_ref=target,
            send_sem=piece_sems.at[at],
            recv_sem=final_sem,
            device_id={"seg": to_seg, "grp": to_grp},
        )
        return own, pltpu.make_async_copy(source, target, final_sem), remote

    @pl.when(core == 1)
    def _():
        @pl.when(is_middle)
        def _():
            start_maps(PARTS[1], False)
            map_groups(PARTS[1], 1, groups, False)
            share_copy().wait_recv()
            shift_copy().wait_recv()

        @pl.when(q > 0)
        def _():
            landed(into_ref, into_sem)

        @pl.when(is_middle)
        def _():
            send_ref[...] = row_times(into_ref[...], map_ref) + shift_in_ref[...]
            copies = chain_copies(q + 1)
            for copy in copies:
                copy.start()
            for copy in copies:
                copy.wait_send()

        for copy in mate_copies():
            copy.wait_send()

    @pl.when(core == 0)
    def _():
        def sum_level(z):
            rows = pl.ds(0, MOST[z])
            landed(plane_in_ref.at[z, :, rows], plane_sems.at[z])
            plane_sum_ref[z, rows] += jnp.sum(plane_in_ref[z, :, rows], axis=0)

            @pl.when(level != z)
            def _():
                line_copy(z).start()

        def line_copy(z):
            at = (z - level + DEPTH - 1) % DEPTH
            return pltpu.make_async_remote_copy(
                src_ref=plane_sum_ref.at[z, 0 : MOST[z]],
                dst_ref=line_in_ref.at[at, 0 : MOST[z]],
                send_sem=line_send_sems.at[z],
                recv_sem=line_sem,
                device_id=lay.device(z, spot, 0),
            )

        def take_level(z):
            coming = line_in_ref.at[:, 0 : MOST[z]]
            landed(coming, line_sem)
            sums = plane_sum_ref[z, 0 : MOST[z]] + jnp.sum(coming[...], axis=0)
            drive_ref[0 : MOST[z], :] = gains_ref[...] * sums
            filler = jnp.zeros((128 - LONGEST, width), F32)
            drive_columns_ref[...] = jnp.transpose(
                jnp.concatenate([drive_ref[...], filler], axis=0)
            )

        def tabulate_all():
            def entry(at, carry):
                tabulate(at)
                return carry

            lax.fori_loop(0, LONGEST // 2, entry, 0)

        def scan_into(row):
            return lax.fori_loop(0, length // 2, recorded, row)

        drive_ref[...] = jnp.zeros_like(drive_ref)
        between_ref[...] = jnp.zeros_like(between_ref)
        states_ref[...] = jnp.zeros_like(states_ref)

        @pl.when(q == 0)
        def _():
            for z in range(2, DEPTH):
                bin_level(z)
            tabulate_all()
            sum_level(0)
            take_level(0)
            send_ref[...] = scan_into(initial_ref[...])
            for copy in chain_copies(1):
                copy.start()
            for z in range(1, DEPTH):
                sum_level(z)
            for copy in chain_copies(1):
                copy.wait_send()

        @pl.when(is_middle)
        def _():
            start_maps(PARTS[0], True)
            for z in range(DEPTH):
                if z + 2 < DEPTH:
                    bin_level(z + 2)
                sum_level(z)
                map_groups(PARTS[0], 1 + z, jnp.minimum(2 + z, groups), True)
            map_groups(PARTS[0], 1 + DEPTH, groups, False)
            share_copy().start()
            tabulate(FIRST + 8 * DEPTH)

        @pl.when(q == n_chip - 1)
        def _():
            for z in range(DEPTH):
                if z + 2 < DEPTH:
                    bin_level(z + 2)
                sum_level(z)
            tabulate_all()

        for z in range(DEPTH):

            @pl.when(jnp.logical_and(level == z, q > 0))
            def _():
                take_level(z)

        @pl.when(is_middle)
        def _():
            shift_ref[...] = lax.fori_loop(0, length // 2, two_steps, jnp.zeros_like(initial_ref))
            shift_copy().start()

        @pl.when(q > 0)
        def _():
            landed(into_ref, into_sem)
            scan_into(into_ref[...])

        before = between_ref[...]
        upper, lower = split(before)
        moved = product(upper, lower, upper_ref[...], lower_ref[...]) + before * diagonal
        between = (moved + drive_ref[...]) * scale_ref[...]
        parity = lax.broadcasted_iota(jnp.int32, (LONGEST, width), 0) % 2
        states_ref[...] = jnp.where(parity == 0, between, states_ref[...])

        def send_piece(at, carry):
            own, local, remote = piece_copies(at)

            @pl.when(own)
            def _():
                local.start()

            @pl.when(jnp.logical_not(own))
            def _():
                remote.start()

            return carry

        lax.fori_loop(0, length // PIECE, send_piece, 0)

        @pl.when(is_middle)
        def _():
            share_copy().wait_send()
            shift_copy().wait_send()

        for z in range(DEPTH):

            @pl.when(level != z)
            def _():
                line_copy(z).wait_send()

        for z in range(DEPTH):
            landed(plane_out_ref.at[z, :, 0 : MOST[z]], plane_send_sems.at[z])

    landed(final_ref, final_sem)
    out_ref[...] = final_ref[...]

    @pl.when(core == 0)
    def _():
        def sent_piece(at, carry):
            own, _, remote = piece_copies(at)

            @pl.when(jnp.logical_not(own))
            def _():
                remote.wait_send()

            return carry

        lax.fori_loop(0, length // PIECE, sent_piece, 0)

    landed(counts_in_ref, counts_sems.at[0])


def filtered(lay, initial, transition, gains, owner, step, tiles):
    n_dev, n_plane = lay.n_seg * lay.n_grp, lay.n_plane
    tile_count, width = tiles.shape
    row = pltpu.VMEM((1, width), F32)
    dma = pltpu.SemaphoreType.DMA
    return pl.pallas_call(
        functools.partial(filter_kernel, lay),
        out_shape=jax.ShapeDtypeStruct((STEP_DEV, width), F32),
        in_specs=[HBM] * 6,
        out_specs=VMEM,
        scratch_shapes=[
            row,
            pltpu.VMEM((width, width), F32),
            row,
            pltpu.VMEM((1, tile_count), jnp.int32),
            pltpu.VMEM((1, tile_count), jnp.int32),
            pltpu.VMEM((1, tile_count), jnp.int32),
            pltpu.VMEM((tile_count, width), F32),
            dma((6,)),
            pltpu.VMEM((width, width), F32),
            pltpu.VMEM((lay.n_chip, 1, 128), F32),
            pltpu.VMEM((width, width), BF16),
            pltpu.VMEM((width, width), BF16),
            pltpu.VMEM((width, width), F32),
            pltpu.VMEM((LONGEST, width), F32),
            pltpu.VMEM((LONGEST, 128), F32),
            pltpu.VMEM((width, 128), F32),
            pltpu.VMEM((LONGEST // 2, width, 128), F32),
            pltpu.VMEM((LONGEST, width), F32),
            pltpu.VMEM((width, 128), F32),
            pltpu.VMEM((LONGEST, width), F32),
            pltpu.VMEM((LONGEST, width), F32),
            pltpu.VMEM((STEP_DEV, width), F32),
            pltpu.VMEM((tile_count, width), F32),
            pltpu.VMEM((1, tile_count), jnp.int32),
            pltpu.VMEM((2 * tile_count, width), BF16),
            pltpu.VMEM((2 * tile_count, width), BF16),
            pltpu.VMEM((n_dev - 1, 1, 128), F32),
            pltpu.VMEM((DEPTH, n_plane - 1, LONGEST, width), F32),
            pltpu.VMEM((DEPTH, n_plane - 1, LONGEST, width), F32),
            pltpu.VMEM((DEPTH, LONGEST, width), F32),
            pltpu.VMEM((DEPTH - 1, LONGEST, width), F32),
            row,
            row,
            row,
            row,
            dma((2,)),
            dma((4,)),
            dma((DEPTH,)),
            dma((DEPTH,)),
            dma((DEPTH,)),
            dma,
            dma((2,)),
            dma((2,)),
            dma,
            dma((2,)),
            dma((LONGEST // PIECE,)),
            dma,
        ],
        compiler_params=pltpu.CompilerParams(
            collective_id=0, has_side_effects=True, vmem_limit_bytes=64 << 20
        ),
    )(initial, transition, gains, owner, step, tiles)


def on_device(initial_state, transition, gains, tiles, tile_owner, tile_step):
    lay = Layout(lax.axis_size("seg"), lax.axis_size("grp"))
    states = filtered(
        lay,
        initial_state[None],
        transition,
        gains[None],
        tile_owner[:, :, 0],
        tile_step,
        tiles[0],
    )
    return states[None]


def solution(mesh):
    in_specs = (P(), P(), P(), P("grp", "seg", None), P("grp", "seg", None), P("grp", "seg"))
    out_specs = P("grp", "seg", None)
    return jax.shard_map(
        on_device, mesh=mesh, in_specs=in_specs, out_specs=out_specs, check_vma=False
    )
```

```python
import functools

import jax
import jax.numpy as jnp
from jax import lax
from jax.experimental import pallas as pl
from jax.experimental.pallas import tpu as pltpu
from jax.sharding import PartitionSpec as P

STEP_DEV = 32
LENGTHS = ((88, 40, 40, 48), (48, 56, 56, 64), (64, 72, 72, 72), (80, 80, 80, 64))
FLAT = sum(LENGTHS, ())
BLOCKS = len(LENGTHS[0])
MOST = tuple(max(lengths) for lengths in LENGTHS)
DEPTH = len(LENGTHS)
LONGEST = max(MOST)
PIECE = 8
PARTS = ((0, 112), (112, 208)), ((208, 368), (368, 512))
SHARE = PARTS[0][-1][1]
FIRST = 7

F32 = jnp.float32
BF16 = jnp.bfloat16
VMEM = pl.BlockSpec(memory_space=pltpu.VMEM)
HBM = pl.BlockSpec(memory_space=pltpu.HBM)


class Layout:
    def __init__(self, n_seg, n_grp):
        self.n_seg, self.n_grp = n_seg, n_grp
        self.n_chip = n_seg * n_grp // 2
        self.n_plane = self.n_chip // DEPTH
        self.core_in_seg = n_seg // DEPTH > n_grp
        self.n_x = n_seg // DEPTH // (2 if self.core_in_seg else 1)

    def turn(self, level, at):
        return at + (self.n_plane - 1 - 2 * at) * (level % 2)

    def device(self, level, spot, core):
        y, x = spot // self.n_x, spot % self.n_x
        x = self.n_x - 1 - x - (self.n_x - 1 - 2 * x) * (y % 2)
        y = self.n_plane // self.n_x - 1 - y
        if self.core_in_seg:
            return {"seg": (level * self.n_x + x) * 2 + core, "grp": y}
        return {"seg": level * self.n_x + x, "grp": y * 2 + core}

    def chip(self, q, core):
        level = q // self.n_plane
        return self.device(level, self.turn(level, q % self.n_plane), core)

    def here(self, seg, grp):
        if self.core_in_seg:
            core, y, across = seg % 2, grp, seg // 2
        else:
            core, y, across = grp % 2, grp // 2, seg
        level, x = across // self.n_x, across % self.n_x
        y = self.n_plane // self.n_x - 1 - y
        x = self.n_x - 1 - x
        x = x + (self.n_x - 1 - 2 * x) * (y % 2)
        return level, y * self.n_x + x, core

    def block(self, q):
        return q * BLOCKS // self.n_plane

    def length(self, q):
        return pick(FLAT, self.block(q))

    def first_step(self, q):
        some = self.n_plane // BLOCKS
        starts = [sum(FLAT[:at]) * some for at in range(len(FLAT))]
        block = self.block(q)
        return pick(starts, block) + (q - block * some) * pick(FLAT, block)

    def index(self, level, spot):
        return level * self.n_plane + self.turn(level, spot)


def pick(table, index):
    if isinstance(index, int):
        return table[index]
    return table[0] + sum((table[at] - table[0]) * (index == at).astype(jnp.int32) for at in range(1, len(table)))


def split(value):
    upper = value.astype(BF16)
    return upper, (value - upper.astype(F32)).astype(BF16)


def product(upper, lower, right_upper, right_lower):
    dot = functools.partial(jnp.dot, preferred_element_type=F32)
    return dot(upper, right_upper) + dot(lower, right_upper) + dot(upper, right_lower)


def stacked_product(upper, lower, right_upper, right_lower):
    dot = functools.partial(jnp.dot, preferred_element_type=F32)
    both = dot(jnp.concatenate([upper, lower], axis=0), right_upper)
    rows = upper.shape[0]
    return both[:rows] + both[rows:] + dot(upper, right_lower)


def row_times(row, matrix_ref):
    depth, width = matrix_ref.shape
    column = jnp.transpose(jnp.broadcast_to(row, (128, depth)))
    return jnp.concatenate(
        [
            jnp.sum(matrix_ref[:, at : at + 128] * column, axis=0, keepdims=True)
            for at in range(0, width, 128)
        ],
        axis=1,
    )


def filter_kernel(
    lay,
    initial_hbm_ref,
    transition_hbm_ref,
    gains_hbm_ref,
    owner_hbm_ref,
    step_hbm_ref,
    tiles_hbm_ref,
    out_ref,
    initial_ref,
    transition_ref,
    gains_ref,
    owner_ref,
    step_ref,
    where_ref,
    tiles_ref,
    load_sems,
    moved_ref,
    counts_ref,
    upper_ref,
    lower_ref,
    map_ref,
    scale_ref,
    column_ref,
    gains_column_ref,
    factors_ref,
    drive_ref,
    drive_columns_ref,
    between_ref,
    states_ref,
    final_ref,
    mate_tiles_ref,
    mate_where_ref,
    tile_upper_ref,
    tile_lower_ref,
    counts_in_ref,
    plane_out_ref,
    plane_in_ref,
    plane_sum_ref,
    line_in_ref,
    into_ref,
    send_ref,
    shift_ref,
    shift_in_ref,
    counts_sems,
    mate_sems,
    plane_send_sems,
    plane_sems,
    line_send_sems,
    line_sem,
    share_sems,
    shift_sems,
    into_sem,
    send_sems,
    piece_sems,
    final_sem,
):
    n_seg, n_grp = lay.n_seg, lay.n_grp
    n_dev, n_plane, n_chip = n_seg * n_grp, lay.n_plane, lay.n_chip
    seg, grp = lax.axis_index("seg"), lax.axis_index("grp")
    level, spot, core = lay.here(seg, grp)
    at_level = lay.turn(level, spot)
    q = level * n_plane + at_level
    me = q * 2 + core
    length = lay.length(q)
    start = lay.first_step(q)
    groups = length // 8
    width = map_ref.shape[1]
    tile_count = tiles_ref.shape[0]
    barrier = pltpu.get_barrier_semaphore()

    def greet(at, carry):
        other = (me + 1 + at) % n_dev
        pl.semaphore_signal(barrier, inc=1, device_id=lay.chip(other // 2, other % 2))
        return carry

    loads = [
        pltpu.make_async_copy(source, target, load_sems.at[at])
        for at, (source, target) in enumerate(
            (
                (owner_hbm_ref, owner_ref),
                (step_hbm_ref, step_ref),
                (tiles_hbm_ref, tiles_ref),
                (transition_hbm_ref, transition_ref),
                (gains_hbm_ref, gains_ref),
                (initial_hbm_ref, initial_ref),
            )
        )
    ]
    for load in loads:
        load.start()
    lax.fori_loop(0, n_dev - 1, greet, 0)

    for load in loads[:2]:
        load.wait()
    where_ref[...] = owner_ref[...] * STEP_DEV + step_ref[...]
    where_columns = jnp.transpose(jnp.broadcast_to(where_ref[...].astype(F32), (128, tile_count)))
    bins = lax.broadcasted_iota(jnp.int32, (1, 128), 1)

    def count(at, carry):
        steps = jnp.where(bins < lay.length(at), bins + lay.first_step(at), -1).astype(F32)
        counts_ref[at] = jnp.sum((where_columns == steps).astype(F32), axis=0, keepdims=True)
        return carry

    lax.fori_loop(0, n_chip, count, 0, unroll=4)
    loads[2].wait()
    pl.semaphore_wait(barrier, n_dev - 1)

    def landed(ref, sem):
        pltpu.make_async_copy(ref, ref, sem).wait()

    def mate_copies():
        return [
            pltpu.make_async_remote_copy(
                src_ref=source,
                dst_ref=target,
                send_sem=mate_sems.at[2 * at],
                recv_sem=mate_sems.at[2 * at + 1],
                device_id=lay.device(level, spot, 0),
            )
            for at, (source, target) in enumerate(
                ((tiles_ref, mate_tiles_ref), (where_ref, mate_where_ref))
            )
        ]

    @pl.when(core == 1)
    def _():
        for copy in mate_copies():
            copy.start()

    def send_counts(at, carry):
        other = (me + 1 + at) % n_dev
        pltpu.make_async_remote_copy(
            src_ref=counts_ref.at[other // 2],
            dst_ref=counts_in_ref.at[at],
            send_sem=counts_sems.at[0],
            recv_sem=counts_sems.at[1],
            device_id=lay.chip(other // 2, other % 2),
        ).start()
        return carry

    lax.fori_loop(0, n_dev - 1, send_counts, 0)

    for load in loads[3:]:
        load.wait()
    moved_ref[...] = jnp.transpose(transition_ref[...])
    row_ids = lax.broadcasted_iota(jnp.int32, (width, width), 0)
    column_ids = lax.broadcasted_iota(jnp.int32, (width, width), 1)
    on_diagonal = row_ids == column_ids
    diagonal = jnp.sum(jnp.where(on_diagonal, moved_ref[...], 0.0), axis=0, keepdims=True)
    upper, lower = split(jnp.where(on_diagonal, 0.0, moved_ref[...]))
    upper_ref[...] = upper
    lower_ref[...] = lower

    def plane_copy(z, spot_to):
        at = (spot_to - spot + n_plane - 1) % n_plane
        return pltpu.make_async_remote_copy(
            src_ref=plane_out_ref.at[z, at, 0 : MOST[z]],
            dst_ref=plane_in_ref.at[z, at, 0 : MOST[z]],
            send_sem=plane_send_sems.at[z],
            recv_sem=plane_sems.at[z],
            device_id=lay.device(level, spot_to, 0),
        )

    def bin_level(z):
        where = jnp.concatenate([where_ref[...], mate_where_ref[...]], axis=1)
        rows = lax.broadcasted_iota(jnp.int32, (MOST[z], 1), 0)
        dot = functools.partial(jnp.dot, preferred_element_type=F32)

        def some(group, carry):
            columns = [group * BLOCKS + ahead for ahead in range(BLOCKS)]
            placed = [
                (rows + lay.first_step(lay.index(z, column)) == where).astype(F32)
                for column in columns
            ]
            placed = jnp.concatenate(placed, axis=0).astype(BF16)
            sums = dot(placed, tile_upper_ref[...]) + dot(placed, tile_lower_ref[...])
            for ahead, column in enumerate(columns):
                part = sums[ahead * MOST[z] : (ahead + 1) * MOST[z]]

                @pl.when(column == spot)
                def _():
                    plane_sum_ref[z, 0 : MOST[z]] = part

                @pl.when(column != spot)
                def _():
                    at = (column - spot + n_plane - 1) % n_plane
                    plane_out_ref[z, at, 0 : MOST[z]] = part
                    plane_copy(z, column).start()

            return carry

        lax.fori_loop(0, n_plane // BLOCKS, some, 0)

    @pl.when(core == 0)
    def _():
        upper, lower = split(tiles_ref[...])
        tile_upper_ref[0:tile_count] = upper
        tile_lower_ref[0:tile_count] = lower
        for copy in mate_copies():
            copy.wait_recv()
        upper, lower = split(mate_tiles_ref[...])
        tile_upper_ref[tile_count:] = upper
        tile_lower_ref[tile_count:] = lower
        bin_level(0)
        bin_level(1)
        gains_column_ref[...] = jnp.transpose(jnp.broadcast_to(gains_ref[...], (128, width)))

    landed(counts_in_ref, counts_sems.at[1])
    counts = counts_ref[q] + jnp.sum(counts_in_ref[...], axis=0)
    column = jnp.transpose(jnp.broadcast_to(counts, (128, 128)))[:LONGEST]
    for at in range(0, width, 128):
        scale_ref[:, at : at + 128] = 1.0 / (1.0 + column * gains_ref[:, at : at + 128])
    column_ref[...] = column

    def tabulate(entry):
        count = column_ref[pl.ds(2 * entry, 1), :]
        whole = 1.0 + count * gains_column_ref[...]
        near = pl.reciprocal(whole, approx=True)
        near = near * (2.0 - whole * near)
        factors_ref[entry] = near * (2.0 - whole * near)

    def advance_maps(parts, first, count, tabled):
        values = [map_ref[begin:end, :] for begin, end in parts]
        for ahead in range(count):
            factor = scale_ref[pl.ds(first + ahead, 1), :]
            for at, value in enumerate(values):
                upper, lower = split(value)
                multiply = stacked_product if parts is PARTS[0] else product
                joined = multiply(upper, lower, upper_ref[...], lower_ref[...])
                values[at] = (joined + value * diagonal) * factor
            if tabled:
                tabulate(first + ahead - 1)
        for (begin, end), value in zip(parts, values):
            map_ref[begin:end, :] = value

    def start_maps(parts, tabled):
        for begin, end in parts:
            map_ref[begin:end, :] = moved_ref[begin:end, :] * scale_ref[pl.ds(0, 1), :]
        advance_maps(parts, 1, FIRST, tabled)

    def map_groups(parts, begin, end, tabled):
        def group(at, carry):
            advance_maps(parts, 8 * at, 8, tabled)
            return carry

        lax.fori_loop(begin, end, group, 0)

    is_middle = jnp.logical_and(q > 0, q < n_chip - 1)

    def chain_copies(q_next):
        return [
            pltpu.make_async_remote_copy(
                src_ref=send_ref,
                dst_ref=into_ref,
                send_sem=send_sems.at[other],
                recv_sem=into_sem,
                device_id=lay.chip(q_next, other),
            )
            for other in (1, 0)
        ]

    share_ref = map_ref.at[0:SHARE]

    def share_copy():
        return pltpu.make_async_remote_copy(
            src_ref=share_ref,
            dst_ref=share_ref,
            send_sem=share_sems.at[0],
            recv_sem=share_sems.at[1],
            device_id=lay.device(level, spot, 1),
        )

    def shift_copy():
        return pltpu.make_async_remote_copy(
            src_ref=shift_ref,
            dst_ref=shift_in_ref,
            send_sem=shift_sems.at[0],
            recv_sem=shift_sems.at[1],
            device_id=lay.device(level, spot, 1),
        )

    lanes = lax.broadcasted_iota(jnp.int32, (width, 128), 1)

    def two_steps(at, row):
        moved = transition_ref[:, 0:128] * row[:, 0:128]
        for block in range(128, width, 128):
            moved += transition_ref[:, block : block + 128] * row[:, block : block + 128]
        moved += jnp.where(lanes == 2 * at, drive_columns_ref[...], 0.0)
        column = jnp.broadcast_to(jnp.sum(moved, axis=1, keepdims=True), (width, 128))
        column *= factors_ref[at]
        row = jnp.concatenate(
            [
                jnp.sum(moved_ref[:, block : block + 128] * column, axis=0, keepdims=True)
                for block in range(0, width, 128)
            ],
            axis=1,
        )
        row += drive_ref[pl.ds(2 * at + 1, 1), :]
        return row * scale_ref[pl.ds(2 * at + 1, 1), :]

    def recorded(at, row):
        between_ref[pl.ds(2 * at, 1), :] = row
        row = two_steps(at, row)
        states_ref[pl.ds(2 * at + 1, 1), :] = row
        return row

    def owner(at):
        step = start + at * PIECE
        window = step // STEP_DEV
        return window % n_seg, window // n_seg, step % STEP_DEV

    def piece_copies(at):
        to_seg, to_grp, row = owner(at)
        own = jnp.logical_and(to_seg == seg, to_grp == grp)
        source = states_ref.at[pl.ds(pl.multiple_of(at * PIECE, PIECE), PIECE)]
        target = final_ref.at[pl.ds(pl.multiple_of(row, PIECE), PIECE)]
        remote = pltpu.make_async_remote_copy(
            src_ref=source,
            dst_ref=target,
            send_sem=piece_sems.at[at],
            recv_sem=final_sem,
            device_id={"seg": to_seg, "grp": to_grp},
        )
        return own, pltpu.make_async_copy(source, target, final_sem), remote

    @pl.when(core == 1)
    def _():
        @pl.when(is_middle)
        def _():
            start_maps(PARTS[1], False)
            map_groups(PARTS[1], 1, groups, False)
            share_copy().wait_recv()
            shift_copy().wait_recv()

        @pl.when(q > 0)
        def _():
            landed(into_ref, into_sem)

        @pl.when(is_middle)
        def _():
            send_ref[...] = row_times(into_ref[...], map_ref) + shift_in_ref[...]
            copies = chain_copies(q + 1)
            for copy in copies:
                copy.start()
            for copy in copies:
                copy.wait_send()

        for copy in mate_copies():
            copy.wait_send()

    @pl.when(core == 0)
    def _():
        def sum_level(z):
            rows = pl.ds(0, MOST[z])
            landed(plane_in_ref.at[z, :, rows], plane_sems.at[z])
            plane_sum_ref[z, rows] += jnp.sum(plane_in_ref[z, :, rows], axis=0)

            @pl.when(level != z)
            def _():
                line_copy(z).start()

        def line_copy(z):
            at = (z - level + DEPTH - 1) % DEPTH
            return pltpu.make_async_remote_copy(
                src_ref=plane_sum_ref.at[z, 0 : MOST[z]],
                dst_ref=line_in_ref.at[at, 0 : MOST[z]],
                send_sem=line_send_sems.at[z],
                recv_sem=line_sem,
                device_id=lay.device(z, spot, 0),
            )

        def take_level(z):
            coming = line_in_ref.at[:, 0 : MOST[z]]
            landed(coming, line_sem)
            sums = plane_sum_ref[z, 0 : MOST[z]] + jnp.sum(coming[...], axis=0)
            drive_ref[0 : MOST[z], :] = gains_ref[...] * sums
            filler = jnp.zeros((128 - LONGEST, width), F32)
            drive_columns_ref[...] = jnp.transpose(
                jnp.concatenate([drive_ref[...], filler], axis=0)
            )

        def tabulate_all():
            def entry(at, carry):
                tabulate(at)
                return carry

            lax.fori_loop(0, LONGEST // 2, entry, 0)

        def scan_into(row):
            return lax.fori_loop(0, length // 2, recorded, row)

        drive_ref[...] = jnp.zeros_like(drive_ref)
        between_ref[...] = jnp.zeros_like(between_ref)
        states_ref[...] = jnp.zeros_like(states_ref)

        @pl.when(q == 0)
        def _():
            for z in range(2, DEPTH):
                bin_level(z)
            tabulate_all()
            sum_level(0)
            take_level(0)
            send_ref[...] = scan_into(initial_ref[...])
            for copy in chain_copies(1):
                copy.start()
            for z in range(1, DEPTH):
                sum_level(z)
            for copy in chain_copies(1):
                copy.wait_send()

        @pl.when(is_middle)
        def _():
            start_maps(PARTS[0], True)
            for z in range(DEPTH):
                if z + 2 < DEPTH:
                    bin_level(z + 2)
                sum_level(z)
                map_groups(PARTS[0], 1 + z, jnp.minimum(2 + z, groups), True)
            map_groups(PARTS[0], 1 + DEPTH, groups, False)
            share_copy().start()
            tabulate(FIRST + 8 * DEPTH)

        @pl.when(q == n_chip - 1)
        def _():
            for z in range(DEPTH):
                if z + 2 < DEPTH:
                    bin_level(z + 2)
                sum_level(z)
            tabulate_all()

        for z in range(DEPTH):

            @pl.when(jnp.logical_and(level == z, q > 0))
            def _():
                take_level(z)

        @pl.when(is_middle)
        def _():
            shift_ref[...] = lax.fori_loop(0, length // 2, two_steps, jnp.zeros_like(initial_ref))
            shift_copy().start()

        @pl.when(q > 0)
        def _():
            landed(into_ref, into_sem)
            scan_into(into_ref[...])

        before = between_ref[...]
        upper, lower = split(before)
        moved = product(upper, lower, upper_ref[...], lower_ref[...]) + before * diagonal
        between = (moved + drive_ref[...]) * scale_ref[...]
        parity = lax.broadcasted_iota(jnp.int32, (LONGEST, width), 0) % 2
        states_ref[...] = jnp.where(parity == 0, between, states_ref[...])

        def send_piece(at, carry):
            own, local, remote = piece_copies(at)

            @pl.when(own)
            def _():
                local.start()

            @pl.when(jnp.logical_not(own))
            def _():
                remote.start()

            return carry

        lax.fori_loop(0, length // PIECE, send_piece, 0)

        @pl.when(is_middle)
        def _():
            share_copy().wait_send()
            shift_copy().wait_send()

        for z in range(DEPTH):

            @pl.when(level != z)
            def _():
                line_copy(z).wait_send()

        for z in range(DEPTH):
            landed(plane_out_ref.at[z, :, 0 : MOST[z]], plane_send_sems.at[z])

    landed(final_ref, final_sem)
    out_ref[...] = final_ref[...]

    @pl.when(core == 0)
    def _():
        def sent_piece(at, carry):
            own, _, remote = piece_copies(at)

            @pl.when(jnp.logical_not(own))
            def _():
                remote.wait_send()

            return carry

        lax.fori_loop(0, length // PIECE, sent_piece, 0)

    landed(counts_in_ref, counts_sems.at[0])


def filtered(lay, initial, transition, gains, owner, step, tiles):
    n_dev, n_plane = lay.n_seg * lay.n_grp, lay.n_plane
    tile_count, width = tiles.shape
    row = pltpu.VMEM((1, width), F32)
    dma = pltpu.SemaphoreType.DMA
    return pl.pallas_call(
        functools.partial(filter_kernel, lay),
        out_shape=jax.ShapeDtypeStruct((STEP_DEV, width), F32),
        in_specs=[HBM] * 6,
        out_specs=VMEM,
        scratch_shapes=[
            row,
            pltpu.VMEM((width, width), F32),
            row,
            pltpu.VMEM((1, tile_count), jnp.int32),
            pltpu.VMEM((1, tile_count), jnp.int32),
            pltpu.VMEM((1, tile_count), jnp.int32),
            pltpu.VMEM((tile_count, width), F32),
            dma((6,)),
            pltpu.VMEM((width, width), F32),
            pltpu.VMEM((lay.n_chip, 1, 128), F32),
            pltpu.VMEM((width, width), BF16),
            pltpu.VMEM((width, width), BF16),
            pltpu.VMEM((width, width), F32),
            pltpu.VMEM((LONGEST, width), F32),
            pltpu.VMEM((LONGEST, 128), F32),
            pltpu.VMEM((width, 128), F32),
            pltpu.VMEM((LONGEST // 2, width, 128), F32),
            pltpu.VMEM((LONGEST, width), F32),
            pltpu.VMEM((width, 128), F32),
            pltpu.VMEM((LONGEST, width), F32),
            pltpu.VMEM((LONGEST, width), F32),
            pltpu.VMEM((STEP_DEV, width), F32),
            pltpu.VMEM((tile_count, width), F32),
            pltpu.VMEM((1, tile_count), jnp.int32),
            pltpu.VMEM((2 * tile_count, width), BF16),
            pltpu.VMEM((2 * tile_count, width), BF16),
            pltpu.VMEM((n_dev - 1, 1, 128), F32),
            pltpu.VMEM((DEPTH, n_plane - 1, LONGEST, width), F32),
            pltpu.VMEM((DEPTH, n_plane - 1, LONGEST, width), F32),
            pltpu.VMEM((DEPTH, LONGEST, width), F32),
            pltpu.VMEM((DEPTH - 1, LONGEST, width), F32),
            row,
            row,
            row,
            row,
            dma((2,)),
            dma((4,)),
            dma((DEPTH,)),
            dma((DEPTH,)),
            dma((DEPTH,)),
            dma,
            dma((2,)),
            dma((2,)),
            dma,
            dma((2,)),
            dma((LONGEST // PIECE,)),
            dma,
        ],
        compiler_params=pltpu.CompilerParams(
            collective_id=0, has_side_effects=True, vmem_limit_bytes=64 << 20
        ),
    )(initial, transition, gains, owner, step, tiles)


def on_device(initial_state, transition, gains, tiles, tile_owner, tile_step):
    lay = Layout(lax.axis_size("seg"), lax.axis_size("grp"))
    states = filtered(
        lay,
        initial_state[None],
        transition,
        gains[None],
        tile_owner[:, :, 0],
        tile_step,
        tiles[0],
    )
    return states[None]


def solution(mesh):
    in_specs = (P(), P(), P(), P("grp", "seg", None), P("grp", "seg", None), P("grp", "seg"))
    out_specs = P("grp", "seg", None)
    return jax.shard_map(
        on_device, mesh=mesh, in_specs=in_specs, out_specs=out_specs, check_vma=False
    )
```
